32 devices in a mesh: seq: 8 (over z, y), mp: 4 (over x, core).
Axes of the slice: x: 2, y: 2, z: 4, core: 2. Of those that a mesh axis runs over, the one named last changes fastest.
Arguments:
- y_first: bfloat16 [2048, 896], P('seq', 'mp'), may hold values from -6 to 6
- y_second: bfloat16 [2048, 896], P('seq', 'mp'), may hold values from -10 to 10
- grad_first: bfloat16 [2048, 896], P('seq', 'mp'), may hold values from -6 to 6
- grad_second: bfloat16 [2048, 896], P('seq', 'mp'), may hold values from -6 to 6
- doc_blocks: int32 [12], replicated, may hold values from 1 to 2, as said below
- last_fill: int32 [12], replicated, may hold values from 1 to 128
- plan: int32 [16], replicated, may hold values from 0 to 15, as said below
- q_weight: bfloat16 [896, 512], P(None, 'mp'), may hold values from -1 to 1
- kv_weight: bfloat16 [2, 896, 128], P(None, 'mp'), may hold values from -1 to 1
- out_weight: bfloat16 [512, 896], P('mp'), may hold values from -0.25 to 0.25
- gate_up: bfloat16 [2, 896, 2560], P(None, None, 'mp'), may hold values from -0.1875 to 0.1875
- down_weight: bfloat16 [2560, 896], P('mp'), may hold values from -0.125 to 0.125
Outputs:
- first_input: bfloat16 [2048, 896], P('seq', 'mp')
- second_input: bfloat16 [2048, 896], P('seq', 'mp')
- first_grad: bfloat16 [2048, 896], P('seq', 'mp')
- second_grad: bfloat16 [2048, 896], P('seq', 'mp')
- q_weight_grad: float32 [896, 512], P('seq', 'mp')
- kv_weight_grad: float32 [2, 896, 128], P(None, 'seq')
- out_weight_grad: float32 [512, 896], P('mp', 'seq')
The draws below stay inside these ranges and needn't reach their ends.
Inputs may be any that keep to these rules, and one draw needn't show every extreme that they name: `doc_blocks`: each document holds 1 or 2 blocks; together they fill all 16 blocks; exactly 4 documents hold 2. A permutation: block b goes to slot plan[b]; slots k * 2 to (k + 1) * 2 - 1 belong to index k of seq; the blocks of one document go to consecutive slots of one index, in order, the first at an even slot.
All inputs are finite; a program needn't handle non-finite values.
Results may differ from the reference program's by a relative error of at most 0.024.
Values may be sent and summed in bfloat16 or wider, within the bound.
A program may use at most 64 MiB of HBM per device.

```python
import math
import jax
import jax.numpy as jnp
from jax import lax

D = 896
HD = 64
QH = 8
KVH = 2
FFW = 2560
BLOCK = 128
SLOTS = 2
TOKENS = 2048
BLOCKS = 16
DOCS = 12
N_SEQ = 8


def layout_draw(key):
    layout_key = jax.random.fold_in(key, 11)
    rank = jax.random.permutation(jax.random.fold_in(layout_key, 1), DOCS).astype(jnp.int32)
    paired = BLOCKS - DOCS
    counts = jnp.where(rank < paired, 2, 1).astype(jnp.int32)
    starts = (jnp.cumsum(counts) - counts).astype(jnp.int32)
    index = jnp.arange(BLOCKS, dtype=jnp.int32)
    owner_doc = (jnp.sum((starts[None, :] <= index[:, None]).astype(jnp.int32), axis=1) - 1).astype(jnp.int32)
    onehot = (owner_doc[:, None] == jnp.arange(DOCS, dtype=jnp.int32)[None, :]).astype(jnp.int32)
    offset = (index - jnp.sum(onehot * starts[None, :], axis=1)).astype(jnp.int32)
    block_rank = jnp.sum(onehot * rank[None, :], axis=1).astype(jnp.int32)
    virtual = jnp.where(block_rank < paired, 2 * block_rank + offset, block_rank + paired).astype(jnp.int32)
    owners = jax.random.permutation(jax.random.fold_in(layout_key, 2), N_SEQ).astype(jnp.int32)
    placed = owners[virtual // SLOTS] * SLOTS + virtual % SLOTS
    return (counts, placed.astype(jnp.int32))


def plant_parts(key):
    plant_key = jax.random.fold_in(key, 31)
    flips = jax.random.bernoulli(jax.random.fold_in(plant_key, 1), 0.5, (D,))
    direction = jnp.where(flips, 1.0, -1.0).astype(jnp.float32) / jnp.sqrt(jnp.float32(D))
    sample = jax.random.normal(jax.random.fold_in(plant_key, 2), (KVH, HD), jnp.float32)
    unit_heads = sample / jnp.sqrt(jnp.sum(sample * sample, axis=1, keepdims=True) / HD)
    factor = jax.random.uniform(jax.random.fold_in(plant_key, 3), (KVH,), jnp.float32, 0.75, 1.0)
    strength = jnp.sqrt(280.0 / (D * jnp.sqrt(jnp.float32(HD))))
    return (direction, unit_heads * (strength * factor)[:, None])


def draw_doc_blocks(key, part):
    return layout_draw(key)[0]


def draw_plan(key, part):
    return layout_draw(key)[1]


def draw_q_weight(key, part):
    direction, planted = plant_parts(key)
    sample = jnp.clip(jax.random.normal(jax.random.fold_in(key, 41), (D, QH * HD), jnp.float32), -4.0, 4.0)
    per_head = jnp.repeat(planted, QH // KVH, axis=0).reshape(QH * HD)
    result = sample / jnp.sqrt(jnp.float32(D)) + direction[:, None] * per_head[None, :]
    return result.astype(jnp.bfloat16)


def draw_kv_weight(key, part):
    direction, planted = plant_parts(key)
    key_part = jnp.clip(jax.random.normal(jax.random.fold_in(key, 43), (KVH, D, HD), jnp.float32), -4.0, 4.0)
    key_part = key_part / jnp.sqrt(jnp.float32(D)) + direction[None, :, None] * planted[:, None, :]
    value_raw = jnp.clip(jax.random.normal(jax.random.fold_in(key, 47), (KVH, D, HD), jnp.float32), -4.0, 4.0)
    value_raw = value_raw / jnp.sqrt(jnp.float32(D))
    along = jnp.einsum('d,cde->ce', direction, value_raw)
    value_part = value_raw - direction[None, :, None] * along[:, None, :]
    return jnp.concatenate([key_part, value_part], axis=2).astype(jnp.bfloat16)


def draw_y_second(key, part):
    stream_key = jax.random.fold_in(key, 23)
    counts, placed = layout_draw(key)
    direction, planted = plant_parts(key)
    signs = direction * jnp.sqrt(jnp.float32(D))
    starts = (jnp.cumsum(counts) - counts).astype(jnp.int32)
    block_index = jnp.arange(BLOCKS, dtype=jnp.int32)
    leading = jnp.sum(((starts[None, :] == block_index[:, None]) & (counts[None, :] == 2)).astype(jnp.int32), axis=1)
    spacing = BLOCK // 4
    offset = jax.random.randint(jax.random.fold_in(stream_key, 1), (BLOCKS,), 0, spacing).astype(jnp.int32)
    within = jnp.arange(BLOCK, dtype=jnp.int32)
    chosen = (within[None, :] % spacing == offset[:, None]) & (leading[:, None] == 1)
    strength = jnp.exp(jax.random.uniform(jax.random.fold_in(stream_key, 2), (BLOCKS,), jnp.float32, jnp.log(2.5), jnp.log(5.0)))
    noise = jnp.clip(jax.random.normal(jax.random.fold_in(stream_key, 3), (BLOCKS * BLOCK, D), jnp.float32), -4.0, 4.0)
    common = noise
    planted_rows = jnp.repeat(strength, BLOCK)[:, None] * signs[None, :] + noise
    result = jnp.where(chosen.reshape(BLOCKS * BLOCK)[:, None], planted_rows, common)
    return result.astype(jnp.bfloat16)


def plant(values, own_key, smallest, largest):
    shape = values.shape
    index_at = [jax.random.randint(jax.random.fold_in(own_key, axis), (), 0, shape[axis]) for axis in range(len(shape))]
    values = values.at[tuple(index_at)].set(smallest)
    longest = shape.index(max(shape))
    index_at[longest] = (index_at[longest] + 1) % shape[longest]
    return values.at[tuple(index_at)].set(largest)


def block_levels(key, shape, pieces, low, largest):
    def one(position, blocks):
        steps = jax.random.uniform(jax.random.fold_in(jax.random.fold_in(key, 6), position), (blocks,), jnp.float32, low / len(pieces), largest / len(pieces))
        return jnp.repeat(jnp.exp(steps), shape[position] // blocks).reshape((-1,) + (1,) * (len(shape) - position - 1))

    loudness = one(*pieces[0])
    for cut in pieces[1:]:
        loudness = loudness * one(*cut)
    return loudness


def normal_values(own_key, shape, width, most, shards=(), held_as=jnp.bfloat16):
    factor_of = block_levels(own_key, shape, shards, -0.22, 0.18) if shards else 1.0
    values = jax.random.normal(own_key, shape, jnp.float32) * width * factor_of
    return jnp.minimum(jnp.maximum(values, -most), most).astype(held_as)


def setup_inputs(seed: int = 0) -> dict:
    splits = jax.random.split(jax.random.key(seed), 13)
    y_first = normal_values(splits[0], (TOKENS, D), 1.0, 6.0, ((0, 8), (1, 4)))
    y_second = draw_y_second(jax.random.fold_in(splits[12], 71), 0)
    grad_first = normal_values(splits[2], (TOKENS, D), 1.0, 6.0, ((0, 8), (1, 4)))
    grad_second = normal_values(splits[3], (TOKENS, D), 1.0, 6.0, ((0, 8), (1, 4)))
    doc_blocks = draw_doc_blocks(jax.random.fold_in(splits[12], 71), 0)
    last_fill = plant(jax.random.randint(splits[5], (DOCS,), 1, BLOCK + 1), jax.random.fold_in(splits[5], 1), 1, BLOCK).astype(jnp.int32)
    plan = draw_plan(jax.random.fold_in(splits[12], 71), 0)
    q_weight = draw_q_weight(jax.random.fold_in(splits[12], 71), 0)
    kv_weight = draw_kv_weight(jax.random.fold_in(splits[12], 71), 0)
    out_weight = normal_values(splits[9], (QH * HD, D), (QH * HD) ** -0.5, 0.25, ((0, 4),))
    gate_up = normal_values(splits[10], (2, D, FFW), D ** -0.5, 0.1875, ((2, 4),))
    down_weight = normal_values(splits[11], (FFW, D), FFW ** -0.5, 0.125, ((0, 4),))
    return dict(y_first=y_first, y_second=y_second, grad_first=grad_first, grad_second=grad_second, doc_blocks=doc_blocks, last_fill=last_fill, plan=plan, q_weight=q_weight, kv_weight=kv_weight, out_weight=out_weight, gate_up=gate_up, down_weight=down_weight)


EPSILON = 1e-06

def normalize(values):
    inverse = lax.rsqrt(lax.optimization_barrier(jnp.mean(values * values, axis=-1, keepdims=True)) + EPSILON)
    return (values * inverse, inverse)

def norm_back(cotangent, normed, inverse):
    inner = lax.optimization_barrier(jnp.mean(cotangent * normed, axis=-1, keepdims=True))
    return (cotangent - normed * inner) * inverse

def block_table(doc_blocks, last_fill, block_count):
    doc_count = doc_blocks.shape[0]
    starts = (jnp.cumsum(doc_blocks) - doc_blocks).astype(jnp.int32)
    index = jnp.arange(block_count, dtype=jnp.int32)
    owner_doc = (lax.optimization_barrier(jnp.sum((starts[None, :] <= index[:, None]).astype(jnp.int32), axis=1)) - 1).astype(jnp.int32)
    onehot = (owner_doc[:, None] == jnp.arange(doc_count, dtype=jnp.int32)[None, :]).astype(jnp.int32)
    first_block = lax.optimization_barrier(jnp.sum(onehot * starts[None, :], axis=1)).astype(jnp.int32)
    length = lax.optimization_barrier(jnp.sum(onehot * doc_blocks[None, :], axis=1)).astype(jnp.int32)
    filled = lax.optimization_barrier(jnp.sum(onehot * last_fill[None, :], axis=1)).astype(jnp.int32)
    limit = jnp.where(index - first_block == length - 1, filled, BLOCK).astype(jnp.int32)
    return (owner_doc, limit)

def attend_mask(doc_rows, valid_rows):
    count = doc_rows.shape[-1]
    order = jnp.arange(count, dtype=jnp.int32)
    causal = order[None, :] <= order[:, None]
    same_doc = doc_rows[..., :, None] == doc_rows[..., None, :]
    keep = valid_rows[..., None, :] | (order[None, :] == order[:, None])
    return same_doc & causal & keep

def masked_softmax(scores, allowed):
    scores = jnp.where(allowed, scores, -1e+30)
    highest = lax.optimization_barrier(jnp.max(scores, axis=-1, keepdims=True))
    expo = jnp.exp(scores - highest)
    return expo / lax.optimization_barrier(jnp.sum(expo, axis=-1, keepdims=True))

def reference(y_first, y_second, grad_first, grad_second, doc_blocks, last_fill, plan, q_weight, kv_weight, out_weight, gate_up, down_weight):
    f32 = jnp.float32
    bf16 = jnp.bfloat16
    block_count = plan.shape[0]
    order = jnp.arange(block_count, dtype=jnp.int32)
    source = jnp.zeros((block_count,), jnp.int32).at[plan].set(order)
    owner_doc, limit = block_table(doc_blocks, last_fill, block_count)
    pair_rows = 2 * BLOCK
    group_count = block_count // 2

    def arrange(values):
        return values.reshape(block_count, BLOCK, D)[source].reshape(group_count, pair_rows, D)
    row_doc = jnp.repeat(owner_doc[source], BLOCK).reshape(group_count, pair_rows)
    row_limit = jnp.repeat(limit[source], BLOCK).reshape(group_count, pair_rows)
    within = jnp.tile(jnp.arange(BLOCK, dtype=jnp.int32), block_count).reshape(group_count, pair_rows)
    valid = within < row_limit
    scale = 1.0 / math.sqrt(HD)
    per_group = QH // KVH

    def step_group(carry, inputs):
        q_acc, kv_acc, out_acc = carry
        first, second, cot_first, cot_second, docs, live = inputs
        n_one, r_one = normalize(first.astype(f32))
        n_one_b = n_one.astype(bf16)
        gate_pre = jnp.dot(n_one_b, gate_up[0], preferred_element_type=f32)
        up_pre = jnp.dot(n_one_b, gate_up[1], preferred_element_type=f32)
        sigma = jax.nn.sigmoid(gate_pre)
        silu_gate = gate_pre * sigma
        hidden = (silu_gate * up_pre).astype(bf16)
        mixed = jnp.dot(hidden, down_weight, preferred_element_type=f32)
        second_in = (second.astype(f32) - mixed).astype(bf16)
        d_hidden = jnp.dot(cot_second, down_weight.T, preferred_element_type=f32)
        d_gate = (d_hidden * up_pre * sigma * (1.0 + gate_pre * (1.0 - sigma))).astype(bf16)
        d_up = (d_hidden * silu_gate).astype(bf16)
        d_norm_one = jnp.dot(d_gate, gate_up[0].T, preferred_element_type=f32) + jnp.dot(d_up, gate_up[1].T, preferred_element_type=f32)
        first_cot = (cot_first.astype(f32) + norm_back(d_norm_one, n_one, r_one)).astype(bf16)
        n_two, r_two = normalize(second_in.astype(f32))
        n_two_b = n_two.astype(bf16)
        query = jnp.dot(n_two_b, q_weight, preferred_element_type=f32).astype(bf16).reshape(pair_rows, QH, HD)
        keyval = jnp.einsum('sk,ckd->scd', n_two_b.astype(f32), kv_weight.astype(f32)).astype(bf16)
        keys = jnp.repeat(keyval[:, :, :HD], per_group, axis=1)
        values = jnp.repeat(keyval[:, :, HD:], per_group, axis=1)
        allowed = attend_mask(docs, live)
        scores = jnp.einsum('ihd,jhd->hij', query.astype(f32), keys.astype(f32)) * scale
        probs = masked_softmax(scores, allowed[None])
        probs_b = probs.astype(bf16)
        heads_out = jnp.einsum('hij,jhd->ihd', probs_b.astype(f32), values.astype(f32)).astype(bf16).reshape(pair_rows, QH * HD)
        attn = jnp.dot(heads_out, out_weight, preferred_element_type=f32)
        first_in = (first.astype(f32) - live[:, None].astype(f32) * attn).astype(bf16)
        masked_cot = first_cot * live[:, None].astype(bf16)
        out_acc = out_acc + jnp.dot(heads_out.T, masked_cot, preferred_element_type=f32)
        d_out = jnp.dot(masked_cot, out_weight.T, preferred_element_type=f32).astype(bf16).reshape(pair_rows, QH, HD)
        d_prob = jnp.einsum('ihd,jhd->hij', d_out.astype(f32), values.astype(f32))
        delta = lax.optimization_barrier(jnp.sum(probs * d_prob, axis=-1, keepdims=True))
        d_score = (probs * (d_prob - delta) * scale).astype(bf16)
        d_query = jnp.einsum('hij,jhd->ihd', d_score.astype(f32), keys.astype(f32)).astype(bf16).reshape(pair_rows, QH * HD)
        d_key = jnp.einsum('hij,ihd->jhd', d_score.astype(f32), query.astype(f32)).astype(bf16).reshape(pair_rows, KVH, per_group, HD)
        d_value = jnp.einsum('hij,ihd->jhd', probs_b.astype(f32), d_out.astype(f32)).astype(bf16).reshape(pair_rows, KVH, per_group, HD)
        q_acc = q_acc + jnp.dot(n_two_b.T, d_query, preferred_element_type=f32)
        key_grad = jnp.einsum('sk,scpd->ckd', n_two_b.astype(f32), d_key.astype(f32))
        value_grad = jnp.einsum('sk,scpd->ckd', n_two_b.astype(f32), d_value.astype(f32))
        kv_acc = kv_acc + jnp.concatenate([key_grad, value_grad], axis=2)
        d_norm_two = jnp.dot(d_query, q_weight.T, preferred_element_type=f32)
        d_norm_two = d_norm_two + jnp.einsum('scpd,ckd->sk', d_key.astype(f32), kv_weight[:, :, :HD].astype(f32))
        d_norm_two = d_norm_two + jnp.einsum('scpd,ckd->sk', d_value.astype(f32), kv_weight[:, :, HD:].astype(f32))
        second_cot = (cot_second.astype(f32) + norm_back(d_norm_two, n_two, r_two)).astype(bf16)
        return ((q_acc, kv_acc, out_acc), (first_in, second_in, first_cot, second_cot))
    start = (jnp.zeros((D, QH * HD), f32), jnp.zeros((KVH, D, 2 * HD), f32), jnp.zeros((QH * HD, D), f32))
    inputs = (arrange(y_first), arrange(y_second), arrange(grad_first), arrange(grad_second), row_doc, valid)
    grads, results = lax.scan(step_group, start, inputs)
    first_in, second_in, first_cot, second_cot = results
    return (first_in.reshape(TOKENS, D), second_in.reshape(TOKENS, D), first_cot.reshape(TOKENS, D), second_cot.reshape(TOKENS, D), grads[0], grads[1], grads[2])
```

```python
import functools
import math

import jax
import jax.numpy as jnp
from jax import lax
from jax.experimental import pallas as pl
from jax.experimental.pallas import tpu as pltpu
from jax.sharding import PartitionSpec as P

BLOCK = 128


EPSILON = 1e-06


def each(start, stop, body):
    if stop - start <= 8:
        for k in range(start, stop):
            body(k)
    else:
        lax.fori_loop(start, stop, lambda k, c: (body(k), c)[1], 0)


def exchange_kernel(plans, *refs):
    count = len(plans)
    sources, targets = refs[:count], refs[count : 2 * count]
    send_sems = refs[2 * count : 3 * count]
    recv_sems = refs[3 * count : 4 * count]
    own_sem = refs[4 * count]
    barrier = pltpu.get_barrier_semaphore()
    sizes = dict((axis, size) for axis, size, _ in plans)
    for axis, size in sizes.items():
        me = lax.axis_index(axis)

        def greet(k):
            pl.semaphore_signal(
                barrier,
                inc=1,
                device_id={axis: lax.rem(me + k, size)},
                device_id_type=pl.DeviceIdType.MESH,
            )

        each(1, size, greet)
    pl.semaphore_wait(barrier, sum(size - 1 for size in sizes.values()))

    def copy_of(i, k):
        axis, size, gather = plans[i]
        me = lax.axis_index(axis)
        peer = lax.rem(me + k, size)
        return pltpu.make_async_remote_copy(
            src_ref=sources[i] if gather else sources[i].at[peer],
            dst_ref=targets[i].at[me],
            send_sem=send_sems[i].at[k],
            recv_sem=recv_sems[i].at[k],
            device_id={axis: peer},
            device_id_type=pl.DeviceIdType.MESH,
        )

    def own_copy(i):
        axis, _, gather = plans[i]
        me = lax.axis_index(axis)
        source = sources[i] if gather else sources[i].at[me]
        return pltpu.make_async_copy(source, targets[i].at[me], own_sem.at[i])

    for i in range(count):
        each(1, plans[i][1], lambda k: copy_of(i, k).start())
        own_copy(i).start()
    for i in range(count):
        each(1, plans[i][1], lambda k: copy_of(i, k).wait())
        own_copy(i).wait()


def exchange(number, *items):
    plans = tuple((axis, lax.axis_size(axis), gather) for _, axis, gather in items)
    arrays = [array for array, _, _ in items]
    shapes = [
        jax.ShapeDtypeStruct((size,) + (a.shape if gather else a.shape[1:]), a.dtype)
        for a, (_, size, gather) in zip(arrays, plans)
    ]
    sems = [pltpu.SemaphoreType.DMA((size,)) for _, size, _ in plans]
    return pl.pallas_call(
        functools.partial(exchange_kernel, plans),
        out_shape=shapes,
        in_specs=[pl.BlockSpec(memory_space=pl.ANY)] * len(arrays),
        out_specs=[pl.BlockSpec(memory_space=pl.ANY)] * len(arrays),
        scratch_shapes=sems + sems + [pltpu.SemaphoreType.DMA((len(arrays),))],
        compiler_params=pltpu.CompilerParams(collective_id=number, has_side_effects=True),
    )(*arrays)


def normalize(values):
    inverse = lax.rsqrt(jnp.mean(values * values, axis=-1, keepdims=True) + EPSILON)
    return (values * inverse, inverse)


def block_table(doc_blocks, last_fill, block_count):
    doc_count = doc_blocks.shape[0]
    starts = jnp.cumsum(doc_blocks) - doc_blocks
    index = jnp.arange(block_count, dtype=jnp.int32)
    owner_doc = jnp.sum((starts[None, :] <= index[:, None]).astype(jnp.int32), axis=1) - 1
    onehot = (owner_doc[:, None] == jnp.arange(doc_count, dtype=jnp.int32)[None, :]).astype(
        jnp.int32
    )
    first_block = jnp.sum(onehot * starts[None, :], axis=1)
    length = jnp.sum(onehot * doc_blocks[None, :], axis=1)
    filled = jnp.sum(onehot * last_fill[None, :], axis=1)
    limit = jnp.where(index - first_block == length - 1, filled, BLOCK)
    return (owner_doc, limit)


def attend_mask(doc_rows, valid_rows):
    count = doc_rows.shape[-1]
    order = jnp.arange(count, dtype=jnp.int32)
    causal = order[None, :] <= order[:, None]
    same_doc = doc_rows[..., :, None] == doc_rows[..., None, :]
    keep = valid_rows[..., None, :] | (order[None, :] == order[:, None])
    return same_doc & causal & keep


def contract_last(left, right):
    return lax.dot_general(
        left, right, (((1,), (1,)), ((), ())), preferred_element_type=jnp.float32
    )


def contract_first(left, right):
    return lax.dot_general(
        left, right, (((0,), (0,)), ((), ())), preferred_element_type=jnp.float32
    )


def to_chunks(values, pieces):
    rows, width = values.shape
    return values.reshape(rows, pieces, width // pieces).transpose(1, 0, 2)


def from_chunks(values):
    pieces, rows, width = values.shape
    return values.transpose(1, 0, 2).reshape(rows, pieces * width)


def total(values):
    return jnp.sum(values.astype(jnp.float32), axis=0)


def shards(
    y_first,
    y_second,
    grad_first,
    grad_second,
    doc_blocks,
    last_fill,
    plan,
    q_weight,
    kv_weight,
    out_weight,
    gate_up,
    down_weight,
):
    f32 = jnp.float32
    bf16 = jnp.bfloat16
    block_count = plan.shape[0]
    seq_size = lax.axis_size("seq")
    mp_size = lax.axis_size("mp")
    order = jnp.arange(block_count, dtype=jnp.int32)
    source = jnp.sum(jnp.where(plan[None, :] == order[:, None], order[None, :], 0), axis=1)
    owner_doc, limit = block_table(doc_blocks, last_fill, block_count)

    row_total, share_width = y_first.shape
    width = share_width * mp_size
    slot_count = row_total // BLOCK
    share_rows = BLOCK // seq_size
    kv_count = kv_weight.shape[0]
    head_size = kv_weight.shape[2] // 2
    local_heads = q_weight.shape[1] // head_size
    per_group = local_heads * mp_size // kv_count
    group_of = [p * local_heads // per_group for p in range(mp_size)]

    streams = jnp.stack(
        [
            item.reshape(slot_count, seq_size, share_rows, share_width).transpose(1, 0, 2, 3)
            for item in (y_first, y_second, grad_first, grad_second)
        ],
        axis=1,
    )
    kv_sent = jnp.stack([kv_weight[g] for g in group_of])
    held, kv_parts = exchange(0, (streams, "seq", False), (kv_sent, "mp", False))
    kv_local = kv_parts.reshape(width, 2 * head_size)
    placed = held[source // slot_count, :, source % slot_count]
    placed = placed.reshape(seq_size, slot_count, 4, share_rows, share_width)
    (owned,) = exchange(1, (placed, "seq", False))
    moved = owned.transpose(2, 1, 0, 3, 4).reshape(4, row_total, share_width)
    gathered = exchange(2, (moved[0], "mp", True), (moved[3], "mp", True))
    first, cot_second = (from_chunks(item) for item in gathered)

    owned_slots = lax.axis_index("seq") * slot_count + jnp.arange(slot_count, dtype=jnp.int32)
    mine = source[owned_slots]
    row_doc = jnp.repeat(owner_doc[mine], BLOCK, total_repeat_length=row_total)
    row_limit = jnp.repeat(limit[mine], BLOCK, total_repeat_length=row_total)
    valid = jnp.arange(row_total, dtype=jnp.int32) % BLOCK < row_limit

    n_one, r_one = normalize(first.astype(f32))
    n_one_b = n_one.astype(bf16)
    gate_pre = jnp.dot(n_one_b, gate_up[0], preferred_element_type=f32)
    up_pre = jnp.dot(n_one_b, gate_up[1], preferred_element_type=f32)
    sigma = jax.nn.sigmoid(gate_pre)
    silu_gate = gate_pre * sigma
    hidden = (silu_gate * up_pre).astype(bf16)
    mix_part = jnp.dot(hidden, down_weight, preferred_element_type=f32).astype(bf16)
    d_hidden = contract_last(cot_second, down_weight)
    d_gate = (d_hidden * up_pre * sigma * (1.0 + gate_pre * (1.0 - sigma))).astype(bf16)
    d_up = (d_hidden * silu_gate).astype(bf16)
    norm_part = contract_last(d_gate, gate_up[0]) + contract_last(d_up, gate_up[1])
    inner_part = jnp.sum(d_gate.astype(f32) * gate_pre + d_up.astype(f32) * up_pre, axis=1)
    mix_got, norm_got, inner_got = exchange(
        3,
        (to_chunks(mix_part, mp_size), "mp", False),
        (to_chunks(norm_part.astype(bf16), mp_size), "mp", False),
        (inner_part.reshape(slot_count, BLOCK), "mp", True),
    )
    second_share = (moved[1].astype(f32) - total(mix_got)).astype(bf16)
    inner = (total(inner_got) / width).reshape(row_total, 1)
    n_one_share = moved[0].astype(f32) * r_one
    first_share = (
        moved[2].astype(f32) + (total(norm_got) - n_one_share * inner) * r_one
    ).astype(bf16)
    second_all, cot_all = exchange(4, (second_share, "mp", True), (first_share, "mp", True))
    second_in = from_chunks(second_all)
    first_cot = from_chunks(cot_all)

    n_two, r_two = normalize(second_in.astype(f32))
    n_two_b = n_two.astype(bf16)
    query_full = jnp.dot(n_two_b, q_weight, preferred_element_type=f32)
    keyval_full = jnp.dot(n_two_b, kv_local, preferred_element_type=f32)
    query = query_full.astype(bf16)
    keyval = keyval_full.astype(bf16)
    pair_rows = 2 * BLOCK
    pair_count = row_total // pair_rows
    query_groups = query.reshape(pair_count, pair_rows, local_heads, head_size)
    key_groups = keyval[:, :head_size].reshape(pair_count, pair_rows, head_size)
    value_groups = keyval[:, head_size:].reshape(pair_count, pair_rows, head_size)
    allowed = attend_mask(
        row_doc.reshape(pair_count, pair_rows), valid.reshape(pair_count, pair_rows)
    )
    scale = 1.0 / math.sqrt(head_size)
    scores = (
        jnp.einsum("gihd,gjd->ghij", query_groups, key_groups, preferred_element_type=f32) * scale
    )
    scores = jnp.where(allowed[:, None], scores, -1e30)
    highest = jnp.max(scores, axis=-1, keepdims=True)
    expo = jnp.exp(scores - highest)
    probs = expo / jnp.sum(expo, axis=-1, keepdims=True)
    probs_b = probs.astype(bf16)
    heads_out = (
        jnp.einsum("ghij,gjd->gihd", probs_b, value_groups, preferred_element_type=f32)
        .astype(bf16)
        .reshape(row_total, local_heads * head_size)
    )
    attn_part = jnp.dot(heads_out, out_weight, preferred_element_type=f32).astype(bf16)
    live = valid[:, None]
    masked_cot = first_cot * live.astype(bf16)
    out_grad = contract_first(masked_cot, heads_out)
    d_out = (
        contract_last(masked_cot, out_weight)
        .astype(bf16)
        .reshape(pair_count, pair_rows, local_heads, head_size)
    )
    d_prob = jnp.einsum("gihd,gjd->ghij", d_out, value_groups, preferred_element_type=f32)
    delta = jnp.sum(probs * d_prob, axis=-1, keepdims=True)
    d_score = (probs * (d_prob - delta) * scale).astype(bf16)
    d_query = (
        jnp.einsum("ghij,gjd->gihd", d_score, key_groups, preferred_element_type=f32)
        .astype(bf16)
        .reshape(row_total, local_heads * head_size)
    )
    d_key = jnp.einsum("ghij,gihd->gjhd", d_score, query_groups, preferred_element_type=f32).astype(
        bf16
    )
    d_value = jnp.einsum("ghij,gihd->gjhd", probs_b, d_out, preferred_element_type=f32).astype(bf16)
    q_grad = contract_first(n_two_b, d_query)
    d_keys = jnp.sum(d_key.astype(f32), axis=2)
    d_values = jnp.sum(d_value.astype(f32), axis=2)
    d_keyval = jnp.concatenate([d_keys, d_values], axis=2).reshape(row_total, 2 * head_size)
    d_keyval_b = d_keyval.astype(bf16)
    kv_own = contract_first(n_two_b, d_keyval_b)
    d_norm_two = contract_last(d_query, q_weight) + contract_last(d_keyval_b, kv_local)
    inner_two_part = jnp.sum(d_query.astype(f32) * query_full, axis=1) + jnp.sum(
        d_keyval * keyval_full, axis=1
    )
    grad_shape = (seq_size, width // seq_size)
    attn_got, norm_two_got, inner_two_got, q_got, kv_got, out_got = exchange(
        5,
        (to_chunks(attn_part, mp_size), "mp", False),
        (to_chunks(d_norm_two.astype(bf16), mp_size), "mp", False),
        (inner_two_part.reshape(slot_count, BLOCK), "mp", True),
        (q_grad.astype(bf16).reshape(grad_shape + q_grad.shape[1:]), "seq", False),
        (kv_own.astype(bf16).reshape(grad_shape + kv_own.shape[1:]), "seq", False),
        (out_grad.astype(bf16).reshape(grad_shape + out_grad.shape[1:]), "seq", False),
    )
    first_in = (moved[0].astype(f32) - live.astype(f32) * total(attn_got)).astype(bf16)
    inner_two = (total(inner_two_got) / width).reshape(row_total, 1)
    n_two_share = second_share.astype(f32) * r_two
    second_cot = (
        moved[3].astype(f32) + (total(norm_two_got) - n_two_share * inner_two) * r_two
    ).astype(bf16)
    (kv_all,) = exchange(6, (total(kv_got), "mp", True))
    kv_share = jnp.stack(
        [
            sum(kv_all[p] for p in range(mp_size) if group_of[p] == g)
            for g in range(kv_count)
        ]
    )
    return (
        first_in,
        second_share,
        first_share,
        second_cot,
        total(q_got),
        kv_share,
        total(out_got).T,
    )


def solution(mesh):
    return jax.shard_map(
        shards,
        mesh=mesh,
        in_specs=(
            P("seq", "mp"),
            P("seq", "mp"),
            P("seq", "mp"),
            P("seq", "mp"),
            P(),
            P(),
            P(),
            P(None, "mp"),
            P(None, "mp", None),
            P("mp", None),
            P(None, None, "mp"),
            P("mp", None),
        ),
        out_specs=(
            P("seq", "mp"),
            P("seq", "mp"),
            P("seq", "mp"),
            P("seq", "mp"),
            P("seq", "mp"),
            P(None, "seq", None),
            P("mp", "seq"),
        ),
        check_vma=False,
    )
```

```python
import functools
import math

import jax
import jax.numpy as jnp
from jax import lax
from jax.experimental import pallas as pl
from jax.experimental.pallas import tpu as pltpu
from jax.sharding import PartitionSpec as P

BLOCK = 128


EPSILON = 1e-06


def each(start, stop, body):
    if stop - start <= 8:
        for k in range(start, stop):
            body(k)
    else:
        lax.fori_loop(start, stop, lambda k, c: (body(k), c)[1], 0)


def near_of(me):
    return me + 1 - 2 * lax.rem(me, 2)


def far_of(me):
    return lax.rem(me + 2, 4)


def remote(source, target, send_sem, recv_sem, axis, peer):
    return pltpu.make_async_remote_copy(
        src_ref=source,
        dst_ref=target,
        send_sem=send_sem,
        recv_sem=recv_sem,
        device_id={axis: peer},
        device_id_type=pl.DeviceIdType.MESH,
    )


def exchange_kernel(plans, *refs):
    count = len(plans)
    sources, targets = refs[:count], refs[count : 2 * count]
    send_sems = refs[2 * count : 3 * count]
    recv_sems = refs[3 * count : 4 * count]
    own_sem = refs[4 * count]
    slots = {}
    rest = list(refs[4 * count + 1 :])
    for i, (_, _, kind) in enumerate(plans):
        if kind == "reduce":
            slots[i] = (rest.pop(0), rest.pop(0))
    direct = [i for i in range(count) if plans[i][2] in ("send", "gather")]
    relays = [i for i in range(count) if plans[i][2] == "relay"]
    reduces = [i for i in range(count) if plans[i][2] == "reduce"]
    barrier = pltpu.get_barrier_semaphore()
    sizes = dict((axis, size) for axis, size, _ in plans)
    for axis, size in sizes.items():
        me = lax.axis_index(axis)

        def greet(k):
            pl.semaphore_signal(
                barrier,
                inc=1,
                device_id={axis: lax.rem(me + k, size)},
                device_id_type=pl.DeviceIdType.MESH,
            )

        each(1, size, greet)
    pl.semaphore_wait(barrier, sum(size - 1 for size in sizes.values()))

    def copy_of(i, k):
        axis, size, kind = plans[i]
        me = lax.axis_index(axis)
        peer = lax.rem(me + k, size)
        source = sources[i] if kind == "gather" else sources[i].at[peer]
        return remote(
            source, targets[i].at[me], send_sems[i].at[k], recv_sems[i].at[k], axis, peer
        )

    def own_copy(i):
        axis, _, kind = plans[i]
        me = lax.axis_index(axis)
        source = sources[i].at[me] if kind == "send" else sources[i]
        return pltpu.make_async_copy(source, targets[i].at[me], own_sem.at[i])

    def relay_copy(i, k):
        axis = plans[i][0]
        me = lax.axis_index(axis)
        peer = far_of(me) if k == 0 else near_of(me)
        source = targets[i].at[far_of(me)] if k == 2 else sources[i]
        target = targets[i].at[far_of(me) if k == 2 else me]
        return remote(source, target, send_sems[i].at[k], recv_sems[i].at[k], axis, peer)

    def reduce_copy(i, k):
        axis = plans[i][0]
        me = lax.axis_index(axis)
        arrived, staged = slots[i]
        if k == 2:
            source, peer = staged, far_of(me)
        else:
            peer = near_of(me)
            source = sources[i].at[far_of(peer) if k == 0 else peer]
        return remote(source, arrived.at[k], send_sems[i].at[k], recv_sems[i].at[k], axis, peer)

    f32 = jnp.float32
    for i in relays:
        relay_copy(i, 0).start()
    for i in reduces:
        reduce_copy(i, 0).start()
    for i in reduces:
        reduce_copy(i, 1).start()
    for i in relays:
        relay_copy(i, 1).start()
        own_copy(i).start()
    for i in direct:
        each(1, plans[i][1], lambda k: copy_of(i, k).start())
        own_copy(i).start()
    for i in reduces:
        arrived, staged = slots[i]
        far = far_of(lax.axis_index(plans[i][0]))
        reduce_copy(i, 0).wait_recv()
        staged[...] = (sources[i][far].astype(f32) + arrived[0].astype(f32)).astype(staged.dtype)
    for i in reduces:
        reduce_copy(i, 2).start()
    for i in relays:
        relay_copy(i, 0).wait_recv()
        relay_copy(i, 2).start()
    for i in reduces:
        arrived, _ = slots[i]
        me = lax.axis_index(plans[i][0])
        reduce_copy(i, 1).wait_recv()
        reduce_copy(i, 2).wait_recv()
        targets[i][...] = (
            sources[i][me].astype(f32) + arrived[1].astype(f32) + arrived[2].astype(f32)
        )
        for k in range(3):
            reduce_copy(i, k).wait_send()
    for i in relays:
        relay_copy(i, 0).wait_send()
        relay_copy(i, 1).wait()
        relay_copy(i, 2).wait()
        own_copy(i).wait()
    for i in direct:
        each(1, plans[i][1], lambda k: copy_of(i, k).wait())
        own_copy(i).wait()


def exchange(number, *items):
    plans, shapes, specs, results, buffers = [], [], [], [], []
    anywhere = pl.BlockSpec(memory_space=pl.ANY)
    inside = pl.BlockSpec(memory_space=pltpu.VMEM)
    summed = []
    for array, axis, kind in items:
        size = lax.axis_size(axis)
        summed.append(kind == "reduce" and size != 4)
        if size != 4:
            kind = {"relay": "gather", "reduce": "send"}.get(kind, kind)
        shape, dtype = array.shape, array.dtype
        if kind in ("relay", "gather"):
            shape = (size,) + shape
        if kind == "reduce":
            shape, dtype = shape[1:], jnp.float32
            buffers += [pltpu.VMEM((3,) + shape, array.dtype), pltpu.VMEM(shape, array.dtype)]
        plans.append((axis, size, kind))
        shapes.append(jax.ShapeDtypeStruct(shape, dtype))
        specs.append(inside if kind == "reduce" else anywhere)
    sems = [pltpu.SemaphoreType.DMA((size,)) for _, size, _ in plans]
    results = pl.pallas_call(
        functools.partial(exchange_kernel, tuple(plans)),
        out_shape=shapes,
        in_specs=specs,
        out_specs=specs,
        scratch_shapes=sems + sems + [pltpu.SemaphoreType.DMA((len(plans),))] + buffers,
        compiler_params=pltpu.CompilerParams(collective_id=number, has_side_effects=True),
    )(*[array for array, _, _ in items])
    return [total(r) if add else r for r, add in zip(results, summed)]


def normalize(values):
    inverse = lax.rsqrt(jnp.mean(values * values, axis=-1, keepdims=True) + EPSILON)
    return (values * inverse, inverse)


def block_table(doc_blocks, last_fill, block_count):
    doc_count = doc_blocks.shape[0]
    starts = jnp.cumsum(doc_blocks) - doc_blocks
    index = jnp.arange(block_count, dtype=jnp.int32)
    owner_doc = jnp.sum((starts[None, :] <= index[:, None]).astype(jnp.int32), axis=1) - 1
    onehot = (owner_doc[:, None] == jnp.arange(doc_count, dtype=jnp.int32)[None, :]).astype(
        jnp.int32
    )
    first_block = jnp.sum(onehot * starts[None, :], axis=1)
    length = jnp.sum(onehot * doc_blocks[None, :], axis=1)
    filled = jnp.sum(onehot * last_fill[None, :], axis=1)
    limit = jnp.where(index - first_block == length - 1, filled, BLOCK)
    return (owner_doc, limit)


def attend_mask(doc_rows, valid_rows):
    count = doc_rows.shape[-1]
    order = jnp.arange(count, dtype=jnp.int32)
    causal = order[None, :] <= order[:, None]
    same_doc = doc_rows[..., :, None] == doc_rows[..., None, :]
    keep = valid_rows[..., None, :] | (order[None, :] == order[:, None])
    return same_doc & causal & keep


def contract_last(left, right):
    return lax.dot_general(
        left, right, (((1,), (1,)), ((), ())), preferred_element_type=jnp.float32
    )


def contract_first(left, right):
    return lax.dot_general(
        left, right, (((0,), (0,)), ((), ())), preferred_element_type=jnp.float32
    )


def to_chunks(values, pieces):
    rows, width = values.shape
    return values.reshape(rows, pieces, width // pieces).transpose(1, 0, 2)


def from_chunks(values):
    pieces, rows, width = values.shape
    return values.transpose(1, 0, 2).reshape(rows, pieces * width)


def total(values):
    return jnp.sum(values.astype(jnp.float32), axis=0)


def shards(
    y_first,
    y_second,
    grad_first,
    grad_second,
    doc_blocks,
    last_fill,
    plan,
    q_weight,
    kv_weight,
    out_weight,
    gate_up,
    down_weight,
):
    f32 = jnp.float32
    bf16 = jnp.bfloat16
    block_count = plan.shape[0]
    seq_size = lax.axis_size("seq")
    mp_size = lax.axis_size("mp")
    order = jnp.arange(block_count, dtype=jnp.int32)
    source = jnp.sum(jnp.where(plan[None, :] == order[:, None], order[None, :], 0), axis=1)
    owner_doc, limit = block_table(doc_blocks, last_fill, block_count)

    row_total, share_width = y_first.shape
    width = share_width * mp_size
    slot_count = row_total // BLOCK
    share_rows = BLOCK // seq_size
    kv_count = kv_weight.shape[0]
    head_size = kv_weight.shape[2] // 2
    local_heads = q_weight.shape[1] // head_size
    per_group = local_heads * mp_size // kv_count
    group_of = [p * local_heads // per_group for p in range(mp_size)]

    def to_shares(*values):
        return jnp.stack(
            [
                item.reshape(slot_count, seq_size, share_rows, share_width).transpose(1, 0, 2, 3)
                for item in values
            ],
            axis=1,
        )

    def to_slots(held):
        placed = held[source // slot_count, :, source % slot_count]
        return placed.reshape(seq_size, slot_count, held.shape[1], share_rows, share_width)

    def from_shares(owned):
        moved = owned.transpose(2, 1, 0, 3, 4)
        return moved.reshape(owned.shape[2], row_total, share_width)

    kv_sent = jnp.stack([kv_weight[g] for g in group_of])
    first_all, cot_second_all, held, kv_parts = exchange(
        0,
        (y_first, "mp", "relay"),
        (grad_second, "mp", "relay"),
        (to_shares(y_first, grad_second), "seq", "send"),
        (kv_sent, "mp", "send"),
    )
    kv_local = kv_parts.reshape(width, 2 * head_size)
    first = from_chunks(first_all)
    cot_second = from_chunks(cot_second_all)

    owned_slots = lax.axis_index("seq") * slot_count + jnp.arange(slot_count, dtype=jnp.int32)
    mine = source[owned_slots]
    row_doc = jnp.repeat(owner_doc[mine], BLOCK, total_repeat_length=row_total)
    row_limit = jnp.repeat(limit[mine], BLOCK, total_repeat_length=row_total)
    valid = jnp.arange(row_total, dtype=jnp.int32) % BLOCK < row_limit

    n_one, r_one = normalize(first.astype(f32))
    n_one_b = n_one.astype(bf16)
    gate_pre = jnp.dot(n_one_b, gate_up[0], preferred_element_type=f32)
    up_pre = jnp.dot(n_one_b, gate_up[1], preferred_element_type=f32)
    sigma = jax.nn.sigmoid(gate_pre)
    silu_gate = gate_pre * sigma
    hidden = (silu_gate * up_pre).astype(bf16)
    mix_part = jnp.dot(hidden, down_weight, preferred_element_type=f32).astype(bf16)
    d_hidden = contract_last(cot_second, down_weight)
    d_gate = (d_hidden * up_pre * sigma * (1.0 + gate_pre * (1.0 - sigma))).astype(bf16)
    d_up = (d_hidden * silu_gate).astype(bf16)
    norm_part = contract_last(d_gate, gate_up[0]) + contract_last(d_up, gate_up[1])
    inner_part = jnp.sum(d_gate.astype(f32) * gate_pre + d_up.astype(f32) * up_pre, axis=1)
    mixed, norm_share, inner_got, owned = exchange(
        1,
        (to_chunks(mix_part, mp_size), "mp", "reduce"),
        (to_chunks(norm_part.astype(bf16), mp_size), "mp", "reduce"),
        (inner_part.reshape(slot_count, BLOCK), "mp", "gather"),
        (to_slots(held), "seq", "send"),
    )
    first_own, cot_second_own = from_shares(owned)
    second_pack = (y_second.astype(f32) - mixed).astype(bf16)
    inner = (total(inner_got) / width).reshape(row_total, 1)
    n_one_share = y_first.astype(f32) * r_one
    first_pack = (
        grad_first.astype(f32) + (norm_share - n_one_share * inner) * r_one
    ).astype(bf16)
    (held,) = exchange(2, (to_shares(second_pack, first_pack), "seq", "send"))
    (owned,) = exchange(3, (to_slots(held), "seq", "send"))
    second_share, first_share = from_shares(owned)
    second_all, cot_all = exchange(4, (second_share, "mp", "relay"), (first_share, "mp", "relay"))
    second_in = from_chunks(second_all)
    first_cot = from_chunks(cot_all)

    n_two, r_two = normalize(second_in.astype(f32))
    n_two_b = n_two.astype(bf16)
    query_full = jnp.dot(n_two_b, q_weight, preferred_element_type=f32)
    keyval_full = jnp.dot(n_two_b, kv_local, preferred_element_type=f32)
    query = query_full.astype(bf16)
    keyval = keyval_full.astype(bf16)
    pair_rows = 2 * BLOCK
    pair_count = row_total // pair_rows
    query_groups = query.reshape(pair_count, pair_rows, local_heads, head_size)
    key_groups = keyval[:, :head_size].reshape(pair_count, pair_rows, head_size)
    value_groups = keyval[:, head_size:].reshape(pair_count, pair_rows, head_size)
    allowed = attend_mask(
        row_doc.reshape(pair_count, pair_rows), valid.reshape(pair_count, pair_rows)
    )
    scale = 1.0 / math.sqrt(head_size)
    scores = (
        jnp.einsum("gihd,gjd->ghij", query_groups, key_groups, preferred_element_type=f32) * scale
    )
    scores = jnp.where(allowed[:, None], scores, -1e30)
    highest = jnp.max(scores, axis=-1, keepdims=True)
    expo = jnp.exp(scores - highest)
    probs = expo / jnp.sum(expo, axis=-1, keepdims=True)
    probs_b = probs.astype(bf16)
    heads_out = (
        jnp.einsum("ghij,gjd->gihd", probs_b, value_groups, preferred_element_type=f32)
        .astype(bf16)
        .reshape(row_total, local_heads * head_size)
    )
    attn_part = jnp.dot(heads_out, out_weight, preferred_element_type=f32).astype(bf16)
    live = valid[:, None]
    masked_cot = first_cot * live.astype(bf16)
    out_grad = contract_first(masked_cot, heads_out)
    d_out = (
        contract_last(masked_cot, out_weight)
        .astype(bf16)
        .reshape(pair_count, pair_rows, local_heads, head_size)
    )
    d_prob = jnp.einsum("gihd,gjd->ghij", d_out, value_groups, preferred_element_type=f32)
    delta = jnp.sum(probs * d_prob, axis=-1, keepdims=True)
    d_score = (probs * (d_prob - delta) * scale).astype(bf16)
    d_query = (
        jnp.einsum("ghij,gjd->gihd", d_score, key_groups, preferred_element_type=f32)
        .astype(bf16)
        .reshape(row_total, local_heads * head_size)
    )
    d_key = jnp.einsum("ghij,gihd->gjhd", d_score, query_groups, preferred_element_type=f32).astype(
        bf16
    )
    d_value = jnp.einsum("ghij,gihd->gjhd", probs_b, d_out, preferred_element_type=f32).astype(bf16)
    q_grad = contract_first(n_two_b, d_query)
    d_keys = jnp.sum(d_key.astype(f32), axis=2)
    d_values = jnp.sum(d_value.astype(f32), axis=2)
    d_keyval = jnp.concatenate([d_keys, d_values], axis=2).reshape(row_total, 2 * head_size)
    d_keyval_b = d_keyval.astype(bf16)
    kv_own = contract_first(n_two_b, d_keyval_b)
    d_norm_two = contract_last(d_query, q_weight) + contract_last(d_keyval_b, kv_local)
    inner_two_part = jnp.sum(d_query.astype(f32) * query_full, axis=1) + jnp.sum(
        d_keyval * keyval_full, axis=1
    )
    grad_shape = (seq_size, width // seq_size)
    attn, norm_two_share, inner_two_got, q_got, kv_got, out_got = exchange(
        5,
        (to_chunks(attn_part, mp_size), "mp", "reduce"),
        (to_chunks(d_norm_two.astype(bf16), mp_size), "mp", "reduce"),
        (inner_two_part.reshape(slot_count, BLOCK), "mp", "gather"),
        (q_grad.astype(bf16).reshape(grad_shape + q_grad.shape[1:]), "seq", "send"),
        (kv_own.astype(bf16).reshape(grad_shape + kv_own.shape[1:]), "seq", "send"),
        (out_grad.astype(bf16).reshape(grad_shape + out_grad.shape[1:]), "seq", "send"),
    )
    first_in = (first_own.astype(f32) - live.astype(f32) * attn).astype(bf16)
    inner_two = (total(inner_two_got) / width).reshape(row_total, 1)
    n_two_share = second_share.astype(f32) * r_two
    second_cot = (
        cot_second_own.astype(f32) + (norm_two_share - n_two_share * inner_two) * r_two
    ).astype(bf16)
    (kv_all,) = exchange(6, (total(kv_got).astype(bf16), "mp", "relay"))
    kv_all = kv_all.astype(f32)
    kv_share = jnp.stack(
        [
            sum(kv_all[p] for p in range(mp_size) if group_of[p] == g)
            for g in range(kv_count)
        ]
    )
    return (
        first_in,
        second_share,
        first_share,
        second_cot,
        total(q_got),
        kv_share,
        total(out_got).T,
    )


def solution(mesh):
    return jax.shard_map(
        shards,
        mesh=mesh,
        in_specs=(
            P("seq", "mp"),
            P("seq", "mp"),
            P("seq", "mp"),
            P("seq", "mp"),
            P(),
            P(),
            P(),
            P(None, "mp"),
            P(None, "mp", None),
            P("mp", None),
            P(None, None, "mp"),
            P("mp", None),
        ),
        out_specs=(
            P("seq", "mp"),
            P("seq", "mp"),
            P("seq", "mp"),
            P("seq", "mp"),
            P("seq", "mp"),
            P(None, "seq", None),
            P("mp", "seq"),
        ),
        check_vma=False,
    )
```

```python
import functools
import math

import jax
import jax.numpy as jnp
from jax import lax
from jax.experimental import pallas as pl
from jax.experimental.pallas import tpu as pltpu
from jax.sharding import PartitionSpec as P

BLOCK = 128


EPSILON = 1e-06


def each(start, stop, body):
    if stop - start <= 8:
        for k in range(start, stop):
            body(k)
    else:
        lax.fori_loop(start, stop, lambda k, c: (body(k), c)[1], 0)


def near_of(me):
    return me + 1 - 2 * lax.rem(me, 2)


def far_of(me):
    return lax.rem(me + 2, 4)


def remote(source, target, send_sem, recv_sem, axis, peer):
    return pltpu.make_async_remote_copy(
        src_ref=source,
        dst_ref=target,
        send_sem=send_sem,
        recv_sem=recv_sem,
        device_id={axis: peer},
        device_id_type=pl.DeviceIdType.MESH,
    )


def exchange_kernel(plans, *refs):
    count = len(plans)
    sources, targets = refs[:count], refs[count : 2 * count]
    send_sems = refs[2 * count : 3 * count]
    recv_sems = refs[3 * count : 4 * count]
    own_sem = refs[4 * count]
    slots = {}
    rest = list(refs[4 * count + 1 :])
    for i, (_, _, kind) in enumerate(plans):
        if kind in ("reduce", "pair"):
            slots[i] = (rest.pop(0), rest.pop(0))
    direct = [i for i in range(count) if plans[i][2] in ("send", "gather")]
    relays = [i for i in range(count) if plans[i][2] == "relay"]
    reduces = [i for i in range(count) if plans[i][2] == "reduce"]
    pairs = [i for i in range(count) if plans[i][2] == "pair"]
    barrier = pltpu.get_barrier_semaphore()
    sizes = dict((axis, size) for axis, size, _ in plans)
    for axis, size in sizes.items():
        me = lax.axis_index(axis)

        def greet(k):
            pl.semaphore_signal(
                barrier,
                inc=1,
                device_id={axis: lax.rem(me + k, size)},
                device_id_type=pl.DeviceIdType.MESH,
            )

        each(1, size, greet)
    pl.semaphore_wait(barrier, sum(size - 1 for size in sizes.values()))

    def copy_of(i, k):
        axis, size, kind = plans[i]
        me = lax.axis_index(axis)
        peer = lax.rem(me + k, size)
        source = sources[i] if kind == "gather" else sources[i].at[peer]
        return remote(
            source, targets[i].at[me], send_sems[i].at[k], recv_sems[i].at[k], axis, peer
        )

    def own_copy(i):
        axis, _, kind = plans[i]
        me = lax.axis_index(axis)
        source = sources[i].at[me] if kind == "send" else sources[i]
        return pltpu.make_async_copy(source, targets[i].at[me], own_sem.at[i])

    def relay_copy(i, k):
        axis = plans[i][0]
        me = lax.axis_index(axis)
        peer = far_of(me) if k == 0 else near_of(me)
        source = targets[i].at[far_of(me)] if k == 2 else sources[i]
        target = targets[i].at[far_of(me) if k == 2 else me]
        return remote(source, target, send_sems[i].at[k], recv_sems[i].at[k], axis, peer)

    def reduce_copy(i, k):
        axis = plans[i][0]
        me = lax.axis_index(axis)
        arrived, staged = slots[i]
        if k == 2:
            source, peer = staged, far_of(me)
        else:
            peer = near_of(me)
            source = sources[i].at[far_of(peer) if k == 0 else peer]
        return remote(source, arrived.at[k], send_sems[i].at[k], recv_sems[i].at[k], axis, peer)

    def near_copy(i, j):
        axis = plans[i][0]
        near = near_of(lax.axis_index(axis))
        arrived, _ = slots[i]
        return remote(
            sources[i].at[2 * j + lax.rem(near, 2)],
            arrived.at[j],
            send_sems[i].at[2 * j],
            recv_sems[i].at[2 * j],
            axis,
            near,
        )

    def pair_copy(i, k):
        axis, size, _ = plans[i]
        me = lax.axis_index(axis)
        peer = lax.rem(me + 2 * k, size)
        _, staged = slots[i]
        return remote(
            staged.at[peer // 2],
            targets[i].at[me // 2],
            send_sems[i].at[2 * k + 1],
            recv_sems[i].at[2 * k + 1],
            axis,
            peer,
        )

    f32 = jnp.float32
    for i in pairs:
        each(0, plans[i][1] // 2, lambda j: near_copy(i, j).start())
    for i in relays:
        relay_copy(i, 0).start()
    for i in reduces:
        reduce_copy(i, 0).start()
    for i in reduces:
        reduce_copy(i, 1).start()
    for i in relays:
        relay_copy(i, 1).start()
        own_copy(i).start()
    for i in direct:
        each(1, plans[i][1], lambda k: copy_of(i, k).start())
        own_copy(i).start()
    for i in reduces:
        arrived, staged = slots[i]
        far = far_of(lax.axis_index(plans[i][0]))
        reduce_copy(i, 0).wait_recv()
        staged[...] = (sources[i][far].astype(f32) + arrived[0].astype(f32)).astype(staged.dtype)
    for i in reduces:
        reduce_copy(i, 2).start()
    for i in relays:
        relay_copy(i, 0).wait_recv()
        relay_copy(i, 2).start()
    for i in pairs:
        arrived, staged = slots[i]
        half = plans[i][1] // 2
        me = lax.axis_index(plans[i][0])

        def add(j):
            near_copy(i, j).wait_recv()
            own = sources[i][2 * j + lax.rem(me, 2)].astype(f32)
            staged[j] = (own + arrived[j].astype(f32)).astype(staged.dtype)

        each(0, half, add)
        each(1, half, lambda k: pair_copy(i, k).start())
    for i in pairs:
        half = plans[i][1] // 2
        me = lax.axis_index(plans[i][0])
        targets[i][me // 2] = slots[i][1][me // 2]
        each(1, half, lambda k: pair_copy(i, k).wait())
        each(0, half, lambda j: near_copy(i, j).wait_send())
    for i in reduces:
        arrived, _ = slots[i]
        me = lax.axis_index(plans[i][0])
        reduce_copy(i, 1).wait_recv()
        reduce_copy(i, 2).wait_recv()
        targets[i][...] = (
            sources[i][me].astype(f32) + arrived[1].astype(f32) + arrived[2].astype(f32)
        )
        for k in range(3):
            reduce_copy(i, k).wait_send()
    for i in relays:
        relay_copy(i, 0).wait_send()
        relay_copy(i, 1).wait()
        relay_copy(i, 2).wait()
        own_copy(i).wait()
    for i in direct:
        each(1, plans[i][1], lambda k: copy_of(i, k).wait())
        own_copy(i).wait()


def exchange(number, *items):
    plans, shapes, specs, results, buffers = [], [], [], [], []
    anywhere = pl.BlockSpec(memory_space=pl.ANY)
    inside = pl.BlockSpec(memory_space=pltpu.VMEM)
    summed = []
    for array, axis, kind in items:
        size = lax.axis_size(axis)
        summed.append(kind == "reduce" and size != 4)
        if size != 4:
            kind = {"relay": "gather", "reduce": "send"}.get(kind, kind)
        shape, dtype = array.shape, array.dtype
        if kind == "pair" and size % 2:
            kind = "send"
        if kind in ("relay", "gather"):
            shape = (size,) + shape
        if kind == "pair":
            shape = (size // 2,) + shape[1:]
            buffers += [pltpu.VMEM(shape, dtype), pltpu.VMEM(shape, dtype)]
        if kind == "reduce":
            shape, dtype = shape[1:], jnp.float32
            buffers += [pltpu.VMEM((3,) + shape, array.dtype), pltpu.VMEM(shape, array.dtype)]
        plans.append((axis, size, kind))
        shapes.append(jax.ShapeDtypeStruct(shape, dtype))
        specs.append(inside if kind in ("reduce", "pair") else anywhere)
    sems = [pltpu.SemaphoreType.DMA((size,)) for _, size, _ in plans]
    results = pl.pallas_call(
        functools.partial(exchange_kernel, tuple(plans)),
        out_shape=shapes,
        in_specs=specs,
        out_specs=specs,
        scratch_shapes=sems + sems + [pltpu.SemaphoreType.DMA((len(plans),))] + buffers,
        compiler_params=pltpu.CompilerParams(collective_id=number, has_side_effects=True),
    )(*[array for array, _, _ in items])
    return [total(r) if add else r for r, add in zip(results, summed)]


def normalize(values):
    inverse = lax.rsqrt(jnp.mean(values * values, axis=-1, keepdims=True) + EPSILON)
    return (values * inverse, inverse)


def block_table(doc_blocks, last_fill, block_count):
    doc_count = doc_blocks.shape[0]
    starts = jnp.cumsum(doc_blocks) - doc_blocks
    index = jnp.arange(block_count, dtype=jnp.int32)
    owner_doc = jnp.sum((starts[None, :] <= index[:, None]).astype(jnp.int32), axis=1) - 1
    onehot = (owner_doc[:, None] == jnp.arange(doc_count, dtype=jnp.int32)[None, :]).astype(
        jnp.int32
    )
    first_block = jnp.sum(onehot * starts[None, :], axis=1)
    length = jnp.sum(onehot * doc_blocks[None, :], axis=1)
    filled = jnp.sum(onehot * last_fill[None, :], axis=1)
    limit = jnp.where(index - first_block == length - 1, filled, BLOCK)
    return (owner_doc, limit)


def attend_mask(doc_rows, valid_rows):
    count = doc_rows.shape[-1]
    order = jnp.arange(count, dtype=jnp.int32)
    causal = order[None, :] <= order[:, None]
    same_doc = doc_rows[..., :, None] == doc_rows[..., None, :]
    keep = valid_rows[..., None, :] | (order[None, :] == order[:, None])
    return same_doc & causal & keep


def contract_last(left, right):
    return lax.dot_general(
        left, right, (((1,), (1,)), ((), ())), preferred_element_type=jnp.float32
    )


def contract_first(left, right):
    return lax.dot_general(
        left, right, (((0,), (0,)), ((), ())), preferred_element_type=jnp.float32
    )


def to_chunks(values, pieces):
    rows, width = values.shape
    return values.reshape(rows, pieces, width // pieces).transpose(1, 0, 2)


def from_chunks(values):
    pieces, rows, width = values.shape
    return values.transpose(1, 0, 2).reshape(rows, pieces * width)


def total(values):
    return jnp.sum(values.astype(jnp.float32), axis=0)


def shards(
    y_first,
    y_second,
    grad_first,
    grad_second,
    doc_blocks,
    last_fill,
    plan,
    q_weight,
    kv_weight,
    out_weight,
    gate_up,
    down_weight,
):
    f32 = jnp.float32
    bf16 = jnp.bfloat16
    block_count = plan.shape[0]
    seq_size = lax.axis_size("seq")
    mp_size = lax.axis_size("mp")
    order = jnp.arange(block_count, dtype=jnp.int32)
    source = jnp.sum(jnp.where(plan[None, :] == order[:, None], order[None, :], 0), axis=1)
    owner_doc, limit = block_table(doc_blocks, last_fill, block_count)

    row_total, share_width = y_first.shape
    width = share_width * mp_size
    slot_count = row_total // BLOCK
    share_rows = BLOCK // seq_size
    kv_count = kv_weight.shape[0]
    head_size = kv_weight.shape[2] // 2
    local_heads = q_weight.shape[1] // head_size
    per_group = local_heads * mp_size // kv_count
    group_of = [p * local_heads // per_group for p in range(mp_size)]

    def to_shares(*values):
        return jnp.stack(
            [
                item.reshape(slot_count, seq_size, share_rows, share_width).transpose(1, 0, 2, 3)
                for item in values
            ],
            axis=1,
        )

    def to_slots(held):
        placed = held[source // slot_count, :, source % slot_count]
        return placed.reshape(seq_size, slot_count, held.shape[1], share_rows, share_width)

    def from_shares(owned):
        moved = owned.transpose(2, 1, 0, 3, 4)
        return moved.reshape(owned.shape[2], row_total, share_width)

    kv_sent = jnp.stack([kv_weight[g] for g in group_of])
    first_all, cot_second_all, held = exchange(
        0,
        (y_first, "mp", "relay"),
        (grad_second, "mp", "relay"),
        (to_shares(y_first, grad_second), "seq", "send"),
    )
    first = from_chunks(first_all)
    cot_second = from_chunks(cot_second_all)

    owned_slots = lax.axis_index("seq") * slot_count + jnp.arange(slot_count, dtype=jnp.int32)
    mine = (plan[None, :] == owned_slots[:, None]).astype(jnp.int32)
    slot_doc = jnp.sum(mine * owner_doc[None, :], axis=1)
    slot_limit = jnp.sum(mine * limit[None, :], axis=1)
    row_doc = jnp.broadcast_to(slot_doc[:, None], (slot_count, BLOCK)).reshape(row_total)
    row_limit = jnp.broadcast_to(slot_limit[:, None], (slot_count, BLOCK)).reshape(row_total)
    valid = jnp.arange(row_total, dtype=jnp.int32) % BLOCK < row_limit

    n_one, r_one = normalize(first.astype(f32))
    n_one_b = n_one.astype(bf16)
    gate_pre = jnp.dot(n_one_b, gate_up[0], preferred_element_type=f32)
    up_pre = jnp.dot(n_one_b, gate_up[1], preferred_element_type=f32)
    sigma = jax.nn.sigmoid(gate_pre)
    silu_gate = gate_pre * sigma
    hidden = (silu_gate * up_pre).astype(bf16)
    mix_part = jnp.dot(hidden, down_weight, preferred_element_type=f32).astype(bf16)
    d_hidden = contract_last(cot_second, down_weight)
    d_gate = (d_hidden * up_pre * sigma * (1.0 + gate_pre * (1.0 - sigma))).astype(bf16)
    d_up = (d_hidden * silu_gate).astype(bf16)
    norm_part = contract_last(d_gate, gate_up[0]) + contract_last(d_up, gate_up[1])
    inner_part = jnp.sum(d_gate.astype(f32) * gate_pre + d_up.astype(f32) * up_pre, axis=1)
    mixed, norm_share, inner_got, owned = exchange(
        1,
        (to_chunks(mix_part, mp_size), "mp", "reduce"),
        (to_chunks(norm_part.astype(bf16), mp_size), "mp", "reduce"),
        (inner_part.reshape(slot_count, BLOCK), "mp", "gather"),
        (to_slots(held), "seq", "send"),
    )
    first_own, cot_second_own = from_shares(owned)
    second_pack = (y_second.astype(f32) - mixed).astype(bf16)
    inner = (total(inner_got) / width).reshape(row_total, 1)
    n_one_share = y_first.astype(f32) * r_one
    first_pack = (
        grad_first.astype(f32) + (norm_share - n_one_share * inner) * r_one
    ).astype(bf16)
    held, kv_parts = exchange(
        2, (to_shares(second_pack, first_pack), "seq", "send"), (kv_sent, "mp", "send")
    )
    kv_local = kv_parts.reshape(width, 2 * head_size)
    (owned,) = exchange(3, (to_slots(held), "seq", "send"))
    second_share, first_share = from_shares(owned)
    second_all, cot_all = exchange(4, (second_share, "mp", "relay"), (first_share, "mp", "relay"))
    second_in = from_chunks(second_all)
    first_cot = from_chunks(cot_all)

    n_two, r_two = normalize(second_in.astype(f32))
    n_two_b = n_two.astype(bf16)
    query_full = jnp.dot(n_two_b, q_weight, preferred_element_type=f32)
    keyval_full = jnp.dot(n_two_b, kv_local, preferred_element_type=f32)
    query = query_full.astype(bf16)
    keyval = keyval_full.astype(bf16)
    pair_rows = 2 * BLOCK
    pair_count = row_total // pair_rows
    query_groups = query.reshape(pair_count, pair_rows, local_heads, head_size)
    key_groups = keyval[:, :head_size].reshape(pair_count, pair_rows, head_size)
    value_groups = keyval[:, head_size:].reshape(pair_count, pair_rows, head_size)
    allowed = attend_mask(
        row_doc.reshape(pair_count, pair_rows), valid.reshape(pair_count, pair_rows)
    )
    scale = 1.0 / math.sqrt(head_size)
    scores = (
        jnp.einsum("gihd,gjd->ghij", query_groups, key_groups, preferred_element_type=f32) * scale
    )
    scores = jnp.where(allowed[:, None], scores, -1e30)
    highest = jnp.max(scores, axis=-1, keepdims=True)
    expo = jnp.exp(scores - highest)
    probs = expo / jnp.sum(expo, axis=-1, keepdims=True)
    probs_b = probs.astype(bf16)
    heads_out = (
        jnp.einsum("ghij,gjd->gihd", probs_b, value_groups, preferred_element_type=f32)
        .astype(bf16)
        .reshape(row_total, local_heads * head_size)
    )
    attn_part = jnp.dot(heads_out, out_weight, preferred_element_type=f32).astype(bf16)
    live = valid[:, None]
    masked_cot = first_cot * live.astype(bf16)
    out_grad = contract_first(masked_cot, heads_out)
    d_out = (
        contract_last(masked_cot, out_weight)
        .astype(bf16)
        .reshape(pair_count, pair_rows, local_heads, head_size)
    )
    d_prob = jnp.einsum("gihd,gjd->ghij", d_out, value_groups, preferred_element_type=f32)
    delta = jnp.sum(probs * d_prob, axis=-1, keepdims=True)
    d_score = (probs * (d_prob - delta) * scale).astype(bf16)
    d_query = (
        jnp.einsum("ghij,gjd->gihd", d_score, key_groups, preferred_element_type=f32)
        .astype(bf16)
        .reshape(row_total, local_heads * head_size)
    )
    d_key = jnp.einsum("ghij,gihd->gjhd", d_score, query_groups, preferred_element_type=f32).astype(
        bf16
    )
    d_value = jnp.einsum("ghij,gihd->gjhd", probs_b, d_out, preferred_element_type=f32).astype(bf16)
    q_grad = contract_first(n_two_b, d_query)
    d_keys = jnp.sum(d_key.astype(f32), axis=2)
    d_values = jnp.sum(d_value.astype(f32), axis=2)
    d_keyval = jnp.concatenate([d_keys, d_values], axis=2).reshape(row_total, 2 * head_size)
    d_keyval_b = d_keyval.astype(bf16)
    kv_own = contract_first(n_two_b, d_keyval_b)
    d_norm_two = contract_last(d_query, q_weight) + contract_last(d_keyval_b, kv_local)
    inner_two_part = jnp.sum(d_query.astype(f32) * query_full, axis=1) + jnp.sum(
        d_keyval * keyval_full, axis=1
    )
    grad_shape = (seq_size, width // seq_size)
    attn, norm_two_share, inner_two_got, q_got, kv_got, out_got = exchange(
        5,
        (to_chunks(attn_part, mp_size), "mp", "reduce"),
        (to_chunks(d_norm_two.astype(bf16), mp_size), "mp", "reduce"),
        (inner_two_part.reshape(slot_count, BLOCK), "mp", "gather"),
        (q_grad.astype(bf16).reshape(grad_shape + q_grad.shape[1:]), "seq", "pair"),
        (kv_own.astype(bf16).reshape(grad_shape + kv_own.shape[1:]), "seq", "pair"),
        (out_grad.astype(bf16).reshape(grad_shape + out_grad.shape[1:]), "seq", "pair"),
    )
    first_in = (first_own.astype(f32) - live.astype(f32) * attn).astype(bf16)
    inner_two = (total(inner_two_got) / width).reshape(row_total, 1)
    n_two_share = second_share.astype(f32) * r_two
    second_cot = (
        cot_second_own.astype(f32) + (norm_two_share - n_two_share * inner_two) * r_two
    ).astype(bf16)
    (kv_all,) = exchange(6, (total(kv_got).astype(bf16), "mp", "relay"))
    kv_all = kv_all.astype(f32)
    kv_share = jnp.stack(
        [
            sum(kv_all[p] for p in range(mp_size) if group_of[p] == g)
            for g in range(kv_count)
        ]
    )
    return (
        first_in,
        second_share,
        first_share,
        second_cot,
        total(q_got),
        kv_share,
        total(out_got).T,
    )


def solution(mesh):
    return jax.shard_map(
        shards,
        mesh=mesh,
        in_specs=(
            P("seq", "mp"),
            P("seq", "mp"),
            P("seq", "mp"),
            P("seq", "mp"),
            P(),
            P(),
            P(),
            P(None, "mp"),
            P(None, "mp", None),
            P("mp", None),
            P(None, None, "mp"),
            P("mp", None),
        ),
        out_specs=(
            P("seq", "mp"),
            P("seq", "mp"),
            P("seq", "mp"),
            P("seq", "mp"),
            P("seq", "mp"),
            P(None, "seq", None),
            P("mp", "seq"),
        ),
        check_vma=False,
    )
```

```python
import functools
import math

import jax
import jax.numpy as jnp
from jax import lax
from jax.experimental import pallas as pl
from jax.experimental.pallas import tpu as pltpu
from jax.sharding import PartitionSpec as P

BLOCK = 128


EPSILON = 1e-06


def each(start, stop, body):
    if stop - start <= 8:
        for k in range(start, stop):
            body(k)
    else:
        lax.fori_loop(start, stop, lambda k, c: (body(k), c)[1], 0)


def near_of(me):
    return me + 1 - 2 * lax.rem(me, 2)


def far_of(me):
    return lax.rem(me + 2, 4)


def remote(source, target, send_sem, recv_sem, axis, peer):
    return pltpu.make_async_remote_copy(
        src_ref=source,
        dst_ref=target,
        send_sem=send_sem,
        recv_sem=recv_sem,
        device_id={axis: peer},
        device_id_type=pl.DeviceIdType.MESH,
    )


def exchange_kernel(plans, *refs):
    count = len(plans)
    sources, targets = refs[:count], refs[count : 2 * count]
    send_sems = refs[2 * count : 3 * count]
    recv_sems = refs[3 * count : 4 * count]
    own_sem = refs[4 * count]
    slots = {}
    rest = list(refs[4 * count + 1 :])
    for i, (_, _, kind) in enumerate(plans):
        if kind in ("reduce", "pair"):
            slots[i] = (rest.pop(0), rest.pop(0))
    direct = [i for i in range(count) if plans[i][2] in ("send", "gather")]
    relays = [i for i in range(count) if plans[i][2] == "relay"]
    reduces = [i for i in range(count) if plans[i][2] == "reduce"]
    pairs = [i for i in range(count) if plans[i][2] == "pair"]
    barrier = pltpu.get_barrier_semaphore()
    sizes = dict((axis, size) for axis, size, _ in plans)
    for axis, size in sizes.items():
        me = lax.axis_index(axis)

        def greet(k):
            pl.semaphore_signal(
                barrier,
                inc=1,
                device_id={axis: lax.rem(me + k, size)},
                device_id_type=pl.DeviceIdType.MESH,
            )

        each(1, size, greet)
    pl.semaphore_wait(barrier, sum(size - 1 for size in sizes.values()))

    def copy_of(i, k):
        axis, size, kind = plans[i]
        me = lax.axis_index(axis)
        peer = lax.rem(me + k, size)
        source = sources[i] if kind == "gather" else sources[i].at[peer]
        return remote(
            source, targets[i].at[me], send_sems[i].at[k], recv_sems[i].at[k], axis, peer
        )

    def own_copy(i):
        axis, _, kind = plans[i]
        me = lax.axis_index(axis)
        source = sources[i].at[me] if kind == "send" else sources[i]
        return pltpu.make_async_copy(source, targets[i].at[me], own_sem.at[i])

    def relay_copy(i, k):
        axis = plans[i][0]
        me = lax.axis_index(axis)
        peer = far_of(me) if k == 0 else near_of(me)
        source = targets[i].at[far_of(me)] if k == 2 else sources[i]
        target = targets[i].at[far_of(me) if k == 2 else me]
        return remote(source, target, send_sems[i].at[k], recv_sems[i].at[k], axis, peer)

    def reduce_copy(i, k):
        axis = plans[i][0]
        me = lax.axis_index(axis)
        arrived, staged = slots[i]
        if k == 2:
            source, peer = staged, far_of(me)
        else:
            peer = near_of(me)
            source = sources[i].at[far_of(peer) if k == 0 else peer]
        return remote(source, arrived.at[k], send_sems[i].at[k], recv_sems[i].at[k], axis, peer)

    def near_copy(i, j):
        axis = plans[i][0]
        near = near_of(lax.axis_index(axis))
        arrived, _ = slots[i]
        return remote(
            sources[i].at[2 * j + lax.rem(near, 2)],
            arrived.at[j],
            send_sems[i].at[2 * j],
            recv_sems[i].at[2 * j],
            axis,
            near,
        )

    def pair_copy(i, k):
        axis, size, _ = plans[i]
        me = lax.axis_index(axis)
        peer = lax.rem(me + 2 * k, size)
        _, staged = slots[i]
        return remote(
            staged.at[peer // 2],
            targets[i].at[me // 2],
            send_sems[i].at[2 * k + 1],
            recv_sems[i].at[2 * k + 1],
            axis,
            peer,
        )

    f32 = jnp.float32
    for i in pairs:
        each(0, plans[i][1] // 2, lambda j: near_copy(i, j).start())
    for i in relays:
        relay_copy(i, 0).start()
    for i in reduces:
        reduce_copy(i, 0).start()
    for i in reduces:
        reduce_copy(i, 1).start()
    for i in relays:
        relay_copy(i, 1).start()
        own_copy(i).start()
    for i in direct:
        each(1, plans[i][1], lambda k: copy_of(i, k).start())
        own_copy(i).start()
    for i in reduces:
        arrived, staged = slots[i]
        far = far_of(lax.axis_index(plans[i][0]))
        reduce_copy(i, 0).wait_recv()
        staged[...] = (sources[i][far].astype(f32) + arrived[0].astype(f32)).astype(staged.dtype)
    for i in reduces:
        reduce_copy(i, 2).start()
    for i in relays:
        relay_copy(i, 0).wait_recv()
        relay_copy(i, 2).start()
    for i in pairs:
        arrived, staged = slots[i]
        half = plans[i][1] // 2
        me = lax.axis_index(plans[i][0])

        def add(j):
            near_copy(i, j).wait_recv()
            own = sources[i][2 * j + lax.rem(me, 2)].astype(f32)
            staged[j] = (own + arrived[j].astype(f32)).astype(staged.dtype)

        each(0, half, add)
        each(1, half, lambda k: pair_copy(i, k).start())
    for i in pairs:
        half = plans[i][1] // 2
        me = lax.axis_index(plans[i][0])
        targets[i][me // 2] = slots[i][1][me // 2]
        each(1, half, lambda k: pair_copy(i, k).wait())
        each(0, half, lambda j: near_copy(i, j).wait_send())
    for i in reduces:
        arrived, _ = slots[i]
        me = lax.axis_index(plans[i][0])
        reduce_copy(i, 1).wait_recv()
        reduce_copy(i, 2).wait_recv()
        targets[i][...] = (
            sources[i][me].astype(f32) + arrived[1].astype(f32) + arrived[2].astype(f32)
        )
        for k in range(3):
            reduce_copy(i, k).wait_send()
    for i in relays:
        relay_copy(i, 0).wait_send()
        relay_copy(i, 1).wait()
        relay_copy(i, 2).wait()
        own_copy(i).wait()
    for i in direct:
        each(1, plans[i][1], lambda k: copy_of(i, k).wait())
        own_copy(i).wait()


def exchange(number, *items):
    plans, shapes, specs, results, buffers = [], [], [], [], []
    anywhere = pl.BlockSpec(memory_space=pl.ANY)
    inside = pl.BlockSpec(memory_space=pltpu.VMEM)
    summed = []
    for array, axis, kind in items:
        size = lax.axis_size(axis)
        summed.append(kind == "reduce" and size != 4)
        if size != 4:
            kind = {"relay": "gather", "reduce": "send"}.get(kind, kind)
        shape, dtype = array.shape, array.dtype
        if kind == "pair" and size % 2:
            kind = "send"
        if kind in ("relay", "gather"):
            shape = (size,) + shape
        if kind == "pair":
            shape = (size // 2,) + shape[1:]
            buffers += [pltpu.VMEM(shape, dtype), pltpu.VMEM(shape, dtype)]
        if kind == "reduce":
            shape, dtype = shape[1:], jnp.float32
            buffers += [pltpu.VMEM((3,) + shape, array.dtype), pltpu.VMEM(shape, array.dtype)]
        plans.append((axis, size, kind))
        shapes.append(jax.ShapeDtypeStruct(shape, dtype))
        specs.append(inside if kind in ("reduce", "pair") else anywhere)
    sems = [pltpu.SemaphoreType.DMA((size,)) for _, size, _ in plans]
    results = pl.pallas_call(
        functools.partial(exchange_kernel, tuple(plans)),
        out_shape=shapes,
        in_specs=specs,
        out_specs=specs,
        scratch_shapes=sems + sems + [pltpu.SemaphoreType.DMA((len(plans),))] + buffers,
        compiler_params=pltpu.CompilerParams(collective_id=number, has_side_effects=True),
    )(*[array for array, _, _ in items])
    return [total(r) if add else r for r, add in zip(results, summed)]


def spread_kernel(size, source, target, send_sem, recv_sem, own_sem):
    me = lax.axis_index("seq")
    part = lax.axis_index("mp")
    near, far = near_of(part), far_of(part)
    barrier = pltpu.get_barrier_semaphore()
    for axis, count in (("seq", size), ("mp", 4)):
        mine = lax.axis_index(axis)

        def greet(k):
            pl.semaphore_signal(
                barrier,
                inc=1,
                device_id={axis: lax.rem(mine + k, count)},
                device_id_type=pl.DeviceIdType.MESH,
            )

        each(1, count, greet)
    pl.semaphore_wait(barrier, size + 2)

    def seq_copy(k):
        peer = lax.rem(me + k, size)
        return remote(
            source.at[peer], target.at[part, me], send_sem.at[k], recv_sem.at[k], "seq", peer
        )

    def pass_copy(k, phase):
        piece = lax.rem(me + size - k, size)
        block = target.at[far if phase == 3 else part, piece]
        place = phase * size + k
        return remote(
            block, block, send_sem.at[place], recv_sem.at[place], "mp", far if phase == 1 else near
        )

    def hand_on(k):
        pass_copy(k, 1).wait_recv()
        pass_copy(k, 3).start()

    def arrive(k):
        seq_copy(k).wait_recv()
        pass_copy(k, 1).start()
        pass_copy(k, 2).start()
        hand_on(k - 1)

    def finish(k):
        pass_copy(k, 1).wait_send()
        pass_copy(k, 2).wait()
        pass_copy(k, 3).wait()

    each(1, size, lambda k: seq_copy(k).start())
    own = pltpu.make_async_copy(source.at[me], target.at[part, me], own_sem)
    own.start()
    own.wait()
    pass_copy(0, 1).start()
    pass_copy(0, 2).start()
    each(1, size, arrive)
    hand_on(size - 1)
    each(0, size, finish)
    each(1, size, lambda k: seq_copy(k).wait_send())


def spread(number, placed):
    size = lax.axis_size("seq")
    if lax.axis_size("mp") != 4:
        (owned,) = exchange(number, (placed, "seq", "send"))
        return exchange(number + 10, (owned, "mp", "gather"))[0]
    anywhere = pl.BlockSpec(memory_space=pl.ANY)
    sems = pltpu.SemaphoreType.DMA((4 * size,))
    return pl.pallas_call(
        functools.partial(spread_kernel, size),
        out_shape=jax.ShapeDtypeStruct((4,) + placed.shape, placed.dtype),
        in_specs=[anywhere],
        out_specs=anywhere,
        scratch_shapes=[sems, sems, pltpu.SemaphoreType.DMA],
        compiler_params=pltpu.CompilerParams(collective_id=number, has_side_effects=True),
    )(placed)


def normalize(values):
    inverse = lax.rsqrt(jnp.mean(values * values, axis=-1, keepdims=True) + EPSILON)
    return (values * inverse, inverse)


def block_table(doc_blocks, last_fill, block_count):
    doc_count = doc_blocks.shape[0]
    starts = jnp.cumsum(doc_blocks) - doc_blocks
    index = jnp.arange(block_count, dtype=jnp.int32)
    owner_doc = jnp.sum((starts[None, :] <= index[:, None]).astype(jnp.int32), axis=1) - 1
    onehot = (owner_doc[:, None] == jnp.arange(doc_count, dtype=jnp.int32)[None, :]).astype(
        jnp.int32
    )
    first_block = jnp.sum(onehot * starts[None, :], axis=1)
    length = jnp.sum(onehot * doc_blocks[None, :], axis=1)
    filled = jnp.sum(onehot * last_fill[None, :], axis=1)
    limit = jnp.where(index - first_block == length - 1, filled, BLOCK)
    return (owner_doc, limit)


def attend_mask(doc_rows, valid_rows):
    count = doc_rows.shape[-1]
    order = jnp.arange(count, dtype=jnp.int32)
    causal = order[None, :] <= order[:, None]
    same_doc = doc_rows[..., :, None] == doc_rows[..., None, :]
    keep = valid_rows[..., None, :] | (order[None, :] == order[:, None])
    return same_doc & causal & keep


def contract_last(left, right):
    return lax.dot_general(
        left, right, (((1,), (1,)), ((), ())), preferred_element_type=jnp.float32
    )


def contract_first(left, right):
    return lax.dot_general(
        left, right, (((0,), (0,)), ((), ())), preferred_element_type=jnp.float32
    )


def to_chunks(values, pieces):
    rows, width = values.shape
    return values.reshape(rows, pieces, width // pieces).transpose(1, 0, 2)


def from_chunks(values):
    pieces, rows, width = values.shape
    return values.transpose(1, 0, 2).reshape(rows, pieces * width)


def total(values):
    return jnp.sum(values.astype(jnp.float32), axis=0)


def shards(
    y_first,
    y_second,
    grad_first,
    grad_second,
    doc_blocks,
    last_fill,
    plan,
    q_weight,
    kv_weight,
    out_weight,
    gate_up,
    down_weight,
):
    f32 = jnp.float32
    bf16 = jnp.bfloat16
    block_count = plan.shape[0]
    seq_size = lax.axis_size("seq")
    mp_size = lax.axis_size("mp")
    order = jnp.arange(block_count, dtype=jnp.int32)
    source = jnp.sum(jnp.where(plan[None, :] == order[:, None], order[None, :], 0), axis=1)
    owner_doc, limit = block_table(doc_blocks, last_fill, block_count)

    row_total, share_width = y_first.shape
    width = share_width * mp_size
    slot_count = row_total // BLOCK
    share_rows = BLOCK // seq_size
    kv_count = kv_weight.shape[0]
    head_size = kv_weight.shape[2] // 2
    local_heads = q_weight.shape[1] // head_size
    per_group = local_heads * mp_size // kv_count
    group_of = [p * local_heads // per_group for p in range(mp_size)]

    def to_shares(*values):
        return jnp.stack(
            [
                item.reshape(slot_count, seq_size, share_rows, share_width).transpose(1, 0, 2, 3)
                for item in values
            ],
            axis=1,
        )

    def to_slots(held):
        placed = held[source // slot_count, :, source % slot_count]
        return placed.reshape(seq_size, slot_count, held.shape[1], share_rows, share_width)

    def from_shares(owned):
        moved = owned.transpose(2, 1, 0, 3, 4)
        return moved.reshape(owned.shape[2], row_total, share_width)

    kv_sent = jnp.stack([kv_weight[g] for g in group_of])
    first_all, cot_second_all, held = exchange(
        0,
        (y_first, "mp", "relay"),
        (grad_second, "mp", "relay"),
        (to_shares(y_first, grad_second), "seq", "send"),
    )
    first = from_chunks(first_all)
    cot_second = from_chunks(cot_second_all)

    owned_slots = lax.axis_index("seq") * slot_count + jnp.arange(slot_count, dtype=jnp.int32)
    mine = (plan[None, :] == owned_slots[:, None]).astype(jnp.int32)
    slot_doc = jnp.sum(mine * owner_doc[None, :], axis=1)
    slot_limit = jnp.sum(mine * limit[None, :], axis=1)
    row_doc = jnp.broadcast_to(slot_doc[:, None], (slot_count, BLOCK)).reshape(row_total)
    row_limit = jnp.broadcast_to(slot_limit[:, None], (slot_count, BLOCK)).reshape(row_total)
    valid = jnp.arange(row_total, dtype=jnp.int32) % BLOCK < row_limit

    n_one, r_one = normalize(first.astype(f32))
    n_one_b = n_one.astype(bf16)
    gate_pre = jnp.dot(n_one_b, gate_up[0], preferred_element_type=f32)
    up_pre = jnp.dot(n_one_b, gate_up[1], preferred_element_type=f32)
    sigma = jax.nn.sigmoid(gate_pre)
    silu_gate = gate_pre * sigma
    hidden = (silu_gate * up_pre).astype(bf16)
    mix_part = jnp.dot(hidden, down_weight, preferred_element_type=f32).astype(bf16)
    d_hidden = contract_last(cot_second, down_weight)
    d_gate = (d_hidden * up_pre * sigma * (1.0 + gate_pre * (1.0 - sigma))).astype(bf16)
    d_up = (d_hidden * silu_gate).astype(bf16)
    norm_part = contract_last(d_gate, gate_up[0]) + contract_last(d_up, gate_up[1])
    inner_part = jnp.sum(d_gate.astype(f32) * gate_pre + d_up.astype(f32) * up_pre, axis=1)
    mixed, norm_share, inner_got, owned = exchange(
        1,
        (to_chunks(mix_part, mp_size), "mp", "reduce"),
        (to_chunks(norm_part.astype(bf16), mp_size), "mp", "reduce"),
        (inner_part.reshape(slot_count, BLOCK), "mp", "gather"),
        (to_slots(held), "seq", "send"),
    )
    first_own, cot_second_own = from_shares(owned)
    second_pack = (y_second.astype(f32) - mixed).astype(bf16)
    inner = (total(inner_got) / width).reshape(row_total, 1)
    n_one_share = y_first.astype(f32) * r_one
    first_pack = (
        grad_first.astype(f32) + (norm_share - n_one_share * inner) * r_one
    ).astype(bf16)
    held, kv_parts = exchange(
        2, (to_shares(second_pack, first_pack), "seq", "send"), (kv_sent, "mp", "send")
    )
    kv_local = kv_parts.reshape(width, 2 * head_size)
    everyone = spread(3, to_slots(held))
    owned = lax.dynamic_index_in_dim(everyone, lax.axis_index("mp"), 0, keepdims=False)
    second_share, first_share = from_shares(owned)
    whole = everyone.transpose(3, 2, 1, 4, 0, 5).reshape(2, row_total, width)
    second_in, first_cot = whole[0], whole[1]

    n_two, r_two = normalize(second_in.astype(f32))
    n_two_b = n_two.astype(bf16)
    query_full = jnp.dot(n_two_b, q_weight, preferred_element_type=f32)
    keyval_full = jnp.dot(n_two_b, kv_local, preferred_element_type=f32)
    query = query_full.astype(bf16)
    keyval = keyval_full.astype(bf16)
    pair_rows = 2 * BLOCK
    pair_count = row_total // pair_rows
    query_groups = query.reshape(pair_count, pair_rows, local_heads, head_size)
    key_groups = keyval[:, :head_size].reshape(pair_count, pair_rows, head_size)
    value_groups = keyval[:, head_size:].reshape(pair_count, pair_rows, head_size)
    allowed = attend_mask(
        row_doc.reshape(pair_count, pair_rows), valid.reshape(pair_count, pair_rows)
    )
    scale = 1.0 / math.sqrt(head_size)
    scores = (
        jnp.einsum("gihd,gjd->ghij", query_groups, key_groups, preferred_element_type=f32) * scale
    )
    scores = jnp.where(allowed[:, None], scores, -1e30)
    highest = jnp.max(scores, axis=-1, keepdims=True)
    expo = jnp.exp(scores - highest)
    probs = expo / jnp.sum(expo, axis=-1, keepdims=True)
    probs_b = probs.astype(bf16)
    heads_out = (
        jnp.einsum("ghij,gjd->gihd", probs_b, value_groups, preferred_element_type=f32)
        .astype(bf16)
        .reshape(row_total, local_heads * head_size)
    )
    attn_part = jnp.dot(heads_out, out_weight, preferred_element_type=f32).astype(bf16)
    live = valid[:, None]
    masked_cot = first_cot * live.astype(bf16)
    out_grad = contract_first(masked_cot, heads_out)
    d_out = (
        contract_last(masked_cot, out_weight)
        .astype(bf16)
        .reshape(pair_count, pair_rows, local_heads, head_size)
    )
    d_prob = jnp.einsum("gihd,gjd->ghij", d_out, value_groups, preferred_element_type=f32)
    delta = jnp.sum(probs * d_prob, axis=-1, keepdims=True)
    d_score = (probs * (d_prob - delta) * scale).astype(bf16)
    d_query = (
        jnp.einsum("ghij,gjd->gihd", d_score, key_groups, preferred_element_type=f32)
        .astype(bf16)
        .reshape(row_total, local_heads * head_size)
    )
    d_key = jnp.einsum("ghij,gihd->gjhd", d_score, query_groups, preferred_element_type=f32).astype(
        bf16
    )
    d_value = jnp.einsum("ghij,gihd->gjhd", probs_b, d_out, preferred_element_type=f32).astype(bf16)
    q_grad = contract_first(n_two_b, d_query)
    d_keys = jnp.sum(d_key.astype(f32), axis=2)
    d_values = jnp.sum(d_value.astype(f32), axis=2)
    d_keyval = jnp.concatenate([d_keys, d_values], axis=2).reshape(row_total, 2 * head_size)
    d_keyval_b = d_keyval.astype(bf16)
    kv_own = contract_first(n_two_b, d_keyval_b)
    d_norm_two = contract_last(d_query, q_weight) + contract_last(d_keyval_b, kv_local)
    inner_two_part = jnp.sum(d_query.astype(f32) * query_full, axis=1) + jnp.sum(
        d_keyval * keyval_full, axis=1
    )
    grad_shape = (seq_size, width // seq_size)
    attn, norm_two_share, inner_two_got, q_got, kv_got, out_got = exchange(
        5,
        (to_chunks(attn_part, mp_size), "mp", "reduce"),
        (to_chunks(d_norm_two.astype(bf16), mp_size), "mp", "reduce"),
        (inner_two_part.reshape(slot_count, BLOCK), "mp", "gather"),
        (q_grad.astype(bf16).reshape(grad_shape + q_grad.shape[1:]), "seq", "pair"),
        (kv_own.astype(bf16).reshape(grad_shape + kv_own.shape[1:]), "seq", "pair"),
        (out_grad.astype(bf16).reshape(grad_shape + out_grad.shape[1:]), "seq", "pair"),
    )
    first_in = (first_own.astype(f32) - live.astype(f32) * attn).astype(bf16)
    inner_two = (total(inner_two_got) / width).reshape(row_total, 1)
    n_two_share = second_share.astype(f32) * r_two
    second_cot = (
        cot_second_own.astype(f32) + (norm_two_share - n_two_share * inner_two) * r_two
    ).astype(bf16)
    (kv_all,) = exchange(6, (total(kv_got).astype(bf16), "mp", "relay"))
    kv_all = kv_all.astype(f32)
    kv_share = jnp.stack(
        [
            sum(kv_all[p] for p in range(mp_size) if group_of[p] == g)
            for g in range(kv_count)
        ]
    )
    return (
        first_in,
        second_share,
        first_share,
        second_cot,
        total(q_got),
        kv_share,
        total(out_got).T,
    )


def solution(mesh):
    return jax.shard_map(
        shards,
        mesh=mesh,
        in_specs=(
            P("seq", "mp"),
            P("seq", "mp"),
            P("seq", "mp"),
            P("seq", "mp"),
            P(),
            P(),
            P(),
            P(None, "mp"),
            P(None, "mp", None),
            P("mp", None),
            P(None, None, "mp"),
            P("mp", None),
        ),
        out_specs=(
            P("seq", "mp"),
            P("seq", "mp"),
            P("seq", "mp"),
            P("seq", "mp"),
            P("seq", "mp"),
            P(None, "seq", None),
            P("mp", "seq"),
        ),
        check_vma=False,
    )
```

```python
import functools
import math

import jax
import jax.numpy as jnp
from jax import lax
from jax.experimental import pallas as pl
from jax.experimental.pallas import tpu as pltpu
from jax.sharding import PartitionSpec as P

BLOCK = 128


EPSILON = 1e-06


def each(start, stop, body):
    if stop - start <= 8:
        for k in range(start, stop):
            body(k)
    else:
        lax.fori_loop(start, stop, lambda k, c: (body(k), c)[1], 0)


def near_of(me):
    return me + 1 - 2 * lax.rem(me, 2)


def far_of(me):
    return lax.rem(me + 2, 4)


def remote(source, target, send_sem, recv_sem, axis, peer):
    return pltpu.make_async_remote_copy(
        src_ref=source,
        dst_ref=target,
        send_sem=send_sem,
        recv_sem=recv_sem,
        device_id={axis: peer},
        device_id_type=pl.DeviceIdType.MESH,
    )


def exchange_kernel(plans, *refs):
    count = len(plans)
    sources, targets = refs[:count], refs[count : 2 * count]
    send_sems = refs[2 * count : 3 * count]
    recv_sems = refs[3 * count : 4 * count]
    own_sem = refs[4 * count]
    slots = {}
    rest = list(refs[4 * count + 1 :])
    for i, (_, _, kind) in enumerate(plans):
        if kind in ("reduce", "pair"):
            slots[i] = (rest.pop(0), rest.pop(0))
    direct = [i for i in range(count) if plans[i][2] in ("send", "gather")]
    relays = [i for i in range(count) if plans[i][2] == "relay"]
    reduces = [i for i in range(count) if plans[i][2] == "reduce"]
    pairs = [i for i in range(count) if plans[i][2] == "pair"]
    barrier = pltpu.get_barrier_semaphore()
    sizes = dict((axis, size) for axis, size, _ in plans)
    for axis, size in sizes.items():
        me = lax.axis_index(axis)

        def greet(k):
            pl.semaphore_signal(
                barrier,
                inc=1,
                device_id={axis: lax.rem(me + k, size)},
                device_id_type=pl.DeviceIdType.MESH,
            )

        each(1, size, greet)
    pl.semaphore_wait(barrier, sum(size - 1 for size in sizes.values()))

    def copy_of(i, k):
        axis, size, kind = plans[i]
        me = lax.axis_index(axis)
        peer = lax.rem(me + k, size)
        source = sources[i] if kind == "gather" else sources[i].at[peer]
        return remote(
            source, targets[i].at[me], send_sems[i].at[k], recv_sems[i].at[k], axis, peer
        )

    def own_copy(i):
        axis, _, kind = plans[i]
        me = lax.axis_index(axis)
        source = sources[i].at[me] if kind == "send" else sources[i]
        return pltpu.make_async_copy(source, targets[i].at[me], own_sem.at[i])

    def relay_copy(i, k):
        axis = plans[i][0]
        me = lax.axis_index(axis)
        peer = far_of(me) if k == 0 else near_of(me)
        source = targets[i].at[far_of(me)] if k == 2 else sources[i]
        target = targets[i].at[far_of(me) if k == 2 else me]
        return remote(source, target, send_sems[i].at[k], recv_sems[i].at[k], axis, peer)

    def reduce_copy(i, k):
        axis = plans[i][0]
        me = lax.axis_index(axis)
        arrived, staged = slots[i]
        if k == 2:
            source, peer = staged, far_of(me)
        else:
            peer = near_of(me)
            source = sources[i].at[far_of(peer) if k == 0 else peer]
        return remote(source, arrived.at[k], send_sems[i].at[k], recv_sems[i].at[k], axis, peer)

    def near_copy(i, j):
        axis = plans[i][0]
        near = near_of(lax.axis_index(axis))
        arrived, _ = slots[i]
        return remote(
            sources[i].at[2 * j + lax.rem(near, 2)],
            arrived.at[j],
            send_sems[i].at[2 * j],
            recv_sems[i].at[2 * j],
            axis,
            near,
        )

    def pair_copy(i, k):
        axis, size, _ = plans[i]
        me = lax.axis_index(axis)
        peer = lax.rem(me + 2 * k, size)
        _, staged = slots[i]
        return remote(
            staged.at[peer // 2],
            targets[i].at[me // 2],
            send_sems[i].at[2 * k + 1],
            recv_sems[i].at[2 * k + 1],
            axis,
            peer,
        )

    f32 = jnp.float32
    for i in pairs:
        each(0, plans[i][1] // 2, lambda j: near_copy(i, j).start())
    for i in relays:
        relay_copy(i, 0).start()
    for i in reduces:
        reduce_copy(i, 0).start()
    for i in reduces:
        reduce_copy(i, 1).start()
    for i in relays:
        relay_copy(i, 1).start()
        own_copy(i).start()
    for i in direct:
        each(1, plans[i][1], lambda k: copy_of(i, k).start())
        own_copy(i).start()
    for i in reduces:
        arrived, staged = slots[i]
        far = far_of(lax.axis_index(plans[i][0]))
        reduce_copy(i, 0).wait_recv()
        staged[...] = (sources[i][far].astype(f32) + arrived[0].astype(f32)).astype(staged.dtype)
    for i in reduces:
        reduce_copy(i, 2).start()
    for i in relays:
        relay_copy(i, 0).wait_recv()
        relay_copy(i, 2).start()
    for i in pairs:
        arrived, staged = slots[i]
        half = plans[i][1] // 2
        me = lax.axis_index(plans[i][0])

        def add(j):
            near_copy(i, j).wait_recv()
            own = sources[i][2 * j + lax.rem(me, 2)].astype(f32)
            staged[j] = (own + arrived[j].astype(f32)).astype(staged.dtype)

        each(0, half, add)
        each(1, half, lambda k: pair_copy(i, k).start())
    for i in pairs:
        half = plans[i][1] // 2
        me = lax.axis_index(plans[i][0])
        targets[i][me // 2] = slots[i][1][me // 2]
        each(1, half, lambda k: pair_copy(i, k).wait())
        each(0, half, lambda j: near_copy(i, j).wait_send())
    for i in reduces:
        arrived, _ = slots[i]
        me = lax.axis_index(plans[i][0])
        reduce_copy(i, 1).wait_recv()
        reduce_copy(i, 2).wait_recv()
        targets[i][...] = (
            sources[i][me].astype(f32) + arrived[1].astype(f32) + arrived[2].astype(f32)
        )
        for k in range(3):
            reduce_copy(i, k).wait_send()
    for i in relays:
        relay_copy(i, 0).wait_send()
        relay_copy(i, 1).wait()
        relay_copy(i, 2).wait()
        own_copy(i).wait()
    for i in direct:
        each(1, plans[i][1], lambda k: copy_of(i, k).wait())
        own_copy(i).wait()


def exchange(number, *items):
    plans, shapes, specs, results, buffers = [], [], [], [], []
    anywhere = pl.BlockSpec(memory_space=pl.ANY)
    inside = pl.BlockSpec(memory_space=pltpu.VMEM)
    summed = []
    for array, axis, kind in items:
        size = lax.axis_size(axis)
        summed.append(kind == "reduce" and size != 4)
        if size != 4:
            kind = {"relay": "gather", "reduce": "send"}.get(kind, kind)
        shape, dtype = array.shape, array.dtype
        if kind == "pair" and size % 2:
            kind = "send"
        if kind in ("relay", "gather"):
            shape = (size,) + shape
        if kind == "pair":
            shape = (size // 2,) + shape[1:]
            buffers += [pltpu.VMEM(shape, dtype), pltpu.VMEM(shape, dtype)]
        if kind == "reduce":
            shape, dtype = shape[1:], jnp.float32
            buffers += [pltpu.VMEM((3,) + shape, array.dtype), pltpu.VMEM(shape, array.dtype)]
        plans.append((axis, size, kind))
        shapes.append(jax.ShapeDtypeStruct(shape, dtype))
        specs.append(inside if kind in ("reduce", "pair") else anywhere)
    sems = [pltpu.SemaphoreType.DMA((size,)) for _, size, _ in plans]
    results = pl.pallas_call(
        functools.partial(exchange_kernel, tuple(plans)),
        out_shape=shapes,
        in_specs=specs,
        out_specs=specs,
        scratch_shapes=sems + sems + [pltpu.SemaphoreType.DMA((len(plans),))] + buffers,
        compiler_params=pltpu.CompilerParams(collective_id=number, has_side_effects=True),
    )(*[array for array, _, _ in items])
    return [total(r) if add else r for r, add in zip(results, summed)]


def normalize(values):
    inverse = lax.rsqrt(jnp.mean(values * values, axis=-1, keepdims=True) + EPSILON)
    return (values * inverse, inverse)


def block_table(doc_blocks, last_fill, block_count):
    doc_count = doc_blocks.shape[0]
    starts = jnp.cumsum(doc_blocks) - doc_blocks
    index = jnp.arange(block_count, dtype=jnp.int32)
    owner_doc = jnp.sum((starts[None, :] <= index[:, None]).astype(jnp.int32), axis=1) - 1
    onehot = (owner_doc[:, None] == jnp.arange(doc_count, dtype=jnp.int32)[None, :]).astype(
        jnp.int32
    )
    first_block = jnp.sum(onehot * starts[None, :], axis=1)
    length = jnp.sum(onehot * doc_blocks[None, :], axis=1)
    filled = jnp.sum(onehot * last_fill[None, :], axis=1)
    limit = jnp.where(index - first_block == length - 1, filled, BLOCK)
    return (owner_doc, limit)


def attend_mask(doc_rows, valid_rows):
    count = doc_rows.shape[-1]
    order = jnp.arange(count, dtype=jnp.int32)
    causal = order[None, :] <= order[:, None]
    same_doc = doc_rows[..., :, None] == doc_rows[..., None, :]
    keep = valid_rows[..., None, :] | (order[None, :] == order[:, None])
    return same_doc & causal & keep


def contract_last(left, right):
    return lax.dot_general(
        left, right, (((1,), (1,)), ((), ())), preferred_element_type=jnp.float32
    )


def contract_first(left, right):
    return lax.dot_general(
        left, right, (((0,), (0,)), ((), ())), preferred_element_type=jnp.float32
    )


def to_chunks(values, pieces):
    rows, width = values.shape
    return values.reshape(rows, pieces, width // pieces).transpose(1, 0, 2)


def from_chunks(values):
    pieces, rows, width = values.shape
    return values.transpose(1, 0, 2).reshape(rows, pieces * width)


def total(values):
    return jnp.sum(values.astype(jnp.float32), axis=0)


def shards(
    y_first,
    y_second,
    grad_first,
    grad_second,
    doc_blocks,
    last_fill,
    plan,
    q_weight,
    kv_weight,
    out_weight,
    gate_up,
    down_weight,
):
    f32 = jnp.float32
    bf16 = jnp.bfloat16
    block_count = plan.shape[0]
    seq_size = lax.axis_size("seq")
    mp_size = lax.axis_size("mp")
    order = jnp.arange(block_count, dtype=jnp.int32)
    source = jnp.sum(jnp.where(plan[None, :] == order[:, None], order[None, :], 0), axis=1)
    owner_doc, limit = block_table(doc_blocks, last_fill, block_count)

    row_total, share_width = y_first.shape
    width = share_width * mp_size
    slot_count = row_total // BLOCK
    share_rows = BLOCK // seq_size
    kv_count = kv_weight.shape[0]
    head_size = kv_weight.shape[2] // 2
    local_heads = q_weight.shape[1] // head_size
    per_group = local_heads * mp_size // kv_count
    group_of = [p * local_heads // per_group for p in range(mp_size)]

    def to_shares(*values):
        return jnp.stack(
            [
                item.reshape(slot_count, seq_size, share_rows, share_width).transpose(1, 0, 2, 3)
                for item in values
            ],
            axis=1,
        )

    def to_slots(held):
        placed = held[source // slot_count, :, source % slot_count]
        return placed.reshape(seq_size, slot_count, held.shape[1], share_rows, share_width)

    def from_shares(owned):
        moved = owned.transpose(2, 1, 0, 3, 4)
        return moved.reshape(owned.shape[2], row_total, share_width)

    kv_sent = jnp.stack([kv_weight[g] for g in group_of])
    first_all, cot_second_all, held = exchange(
        0,
        (y_first, "mp", "relay"),
        (grad_second, "mp", "relay"),
        (to_shares(y_first, grad_second), "seq", "send"),
    )
    first = from_chunks(first_all)
    cot_second = from_chunks(cot_second_all)

    owned_slots = lax.axis_index("seq") * slot_count + jnp.arange(slot_count, dtype=jnp.int32)
    mine = (plan[None, :] == owned_slots[:, None]).astype(jnp.int32)
    slot_doc = jnp.sum(mine * owner_doc[None, :], axis=1)
    slot_limit = jnp.sum(mine * limit[None, :], axis=1)
    row_doc = jnp.broadcast_to(slot_doc[:, None], (slot_count, BLOCK)).reshape(row_total)
    row_limit = jnp.broadcast_to(slot_limit[:, None], (slot_count, BLOCK)).reshape(row_total)
    valid = jnp.arange(row_total, dtype=jnp.int32) % BLOCK < row_limit

    n_one, r_one = normalize(first.astype(f32))
    n_one_b = n_one.astype(bf16)
    gate_pre = jnp.dot(n_one_b, gate_up[0], preferred_element_type=f32)
    up_pre = jnp.dot(n_one_b, gate_up[1], preferred_element_type=f32)
    sigma = jax.nn.sigmoid(gate_pre)
    silu_gate = gate_pre * sigma
    hidden = (silu_gate * up_pre).astype(bf16)
    mix_part = jnp.dot(hidden, down_weight, preferred_element_type=f32).astype(bf16)
    d_hidden = contract_last(cot_second, down_weight)
    d_gate = (d_hidden * up_pre * sigma * (1.0 + gate_pre * (1.0 - sigma))).astype(bf16)
    d_up = (d_hidden * silu_gate).astype(bf16)
    norm_part = contract_last(d_gate, gate_up[0]) + contract_last(d_up, gate_up[1])
    inner_part = jnp.sum(d_gate.astype(f32) * gate_pre + d_up.astype(f32) * up_pre, axis=1)
    mixed, norm_share, inner_got, owned = exchange(
        1,
        (to_chunks(mix_part, mp_size), "mp", "reduce"),
        (to_chunks(norm_part.astype(bf16), mp_size), "mp", "reduce"),
        (inner_part.reshape(slot_count, BLOCK), "mp", "gather"),
        (to_slots(held), "seq", "send"),
    )
    first_own, cot_second_own = from_shares(owned)
    second_pack = (y_second.astype(f32) - mixed).astype(bf16)
    inner = (total(inner_got) / width).reshape(row_total, 1)
    n_one_share = y_first.astype(f32) * r_one
    first_pack = (
        grad_first.astype(f32) + (norm_share - n_one_share * inner) * r_one
    ).astype(bf16)
    held, kv_parts = exchange(
        2, (to_shares(second_pack, first_pack), "seq", "send"), (kv_sent, "mp", "send")
    )
    kv_local = kv_parts.reshape(width, 2 * head_size)
    (owned,) = exchange(3, (to_slots(held), "seq", "send"))
    second_share, first_share = from_shares(owned)
    second_all, cot_all = exchange(4, (second_share, "mp", "relay"), (first_share, "mp", "relay"))
    second_in = from_chunks(second_all)
    first_cot = from_chunks(cot_all)

    n_two, r_two = normalize(second_in.astype(f32))
    n_two_b = n_two.astype(bf16)
    query_full = jnp.dot(n_two_b, q_weight, preferred_element_type=f32)
    keyval_full = jnp.dot(n_two_b, kv_local, preferred_element_type=f32)
    query = query_full.astype(bf16)
    keyval = keyval_full.astype(bf16)
    pair_rows = 2 * BLOCK
    pair_count = row_total // pair_rows
    query_groups = query.reshape(pair_count, pair_rows, local_heads, head_size)
    key_groups = keyval[:, :head_size].reshape(pair_count, pair_rows, head_size)
    value_groups = keyval[:, head_size:].reshape(pair_count, pair_rows, head_size)
    allowed = attend_mask(
        row_doc.reshape(pair_count, pair_rows), valid.reshape(pair_count, pair_rows)
    )
    scale = 1.0 / math.sqrt(head_size)
    scores = (
        jnp.einsum("gihd,gjd->ghij", query_groups, key_groups, preferred_element_type=f32) * scale
    )
    scores = jnp.where(allowed[:, None], scores, -1e30)
    highest = jnp.max(scores, axis=-1, keepdims=True)
    expo = jnp.exp(scores - highest)
    probs = expo / jnp.sum(expo, axis=-1, keepdims=True)
    probs_b = probs.astype(bf16)
    heads_out = (
        jnp.einsum("ghij,gjd->gihd", probs_b, value_groups, preferred_element_type=f32)
        .astype(bf16)
        .reshape(row_total, local_heads * head_size)
    )
    attn_part = jnp.dot(heads_out, out_weight, preferred_element_type=f32).astype(bf16)
    live = valid[:, None]
    masked_cot = first_cot * live.astype(bf16)
    out_grad = contract_first(masked_cot, heads_out)
    d_out = (
        contract_last(masked_cot, out_weight)
        .astype(bf16)
        .reshape(pair_count, pair_rows, local_heads, head_size)
    )
    d_prob = jnp.einsum("gihd,gjd->ghij", d_out, value_groups, preferred_element_type=f32)
    delta = jnp.sum(probs * d_prob, axis=-1, keepdims=True)
    d_score = (probs * (d_prob - delta) * scale).astype(bf16)
    d_query = (
        jnp.einsum("ghij,gjd->gihd", d_score, key_groups, preferred_element_type=f32)
        .astype(bf16)
        .reshape(row_total, local_heads * head_size)
    )
    d_key = jnp.einsum("ghij,gihd->gjhd", d_score, query_groups, preferred_element_type=f32).astype(
        bf16
    )
    d_value = jnp.einsum("ghij,gihd->gjhd", probs_b, d_out, preferred_element_type=f32).astype(bf16)
    q_grad = contract_first(n_two_b, d_query)
    d_keys = jnp.sum(d_key.astype(f32), axis=2)
    d_values = jnp.sum(d_value.astype(f32), axis=2)
    d_keyval = jnp.concatenate([d_keys, d_values], axis=2).reshape(row_total, 2 * head_size)
    d_keyval_b = d_keyval.astype(bf16)
    kv_own = contract_first(n_two_b, d_keyval_b)
    d_norm_two = contract_last(d_query, q_weight) + contract_last(d_keyval_b, kv_local)
    inner_two_part = jnp.sum(d_query.astype(f32) * query_full, axis=1) + jnp.sum(
        d_keyval * keyval_full, axis=1
    )
    grad_shape = (seq_size, width // seq_size)
    attn, norm_two_share, inner_two_got, q_got, kv_got, out_got = exchange(
        5,
        (to_chunks(attn_part, mp_size), "mp", "reduce"),
        (to_chunks(d_norm_two.astype(bf16), mp_size), "mp", "reduce"),
        (inner_two_part.reshape(slot_count, BLOCK), "mp", "gather"),
        (q_grad.astype(bf16).reshape(grad_shape + q_grad.shape[1:]), "seq", "pair"),
        (kv_own.astype(bf16).reshape(grad_shape + kv_own.shape[1:]), "seq", "pair"),
        (out_grad.astype(bf16).reshape(grad_shape + out_grad.shape[1:]), "seq", "pair"),
    )
    first_in = (first_own.astype(f32) - live.astype(f32) * attn).astype(bf16)
    inner_two = (total(inner_two_got) / width).reshape(row_total, 1)
    n_two_share = second_share.astype(f32) * r_two
    second_cot = (
        cot_second_own.astype(f32) + (norm_two_share - n_two_share * inner_two) * r_two
    ).astype(bf16)
    (kv_all,) = exchange(6, (total(kv_got).astype(bf16), "mp", "gather"))
    kv_all = kv_all.astype(f32)
    kv_share = jnp.stack(
        [
            sum(kv_all[p] for p in range(mp_size) if group_of[p] == g)
            for g in range(kv_count)
        ]
    )
    return (
        first_in,
        second_share,
        first_share,
        second_cot,
        total(q_got),
        kv_share,
        total(out_got).T,
    )


def solution(mesh):
    return jax.shard_map(
        shards,
        mesh=mesh,
        in_specs=(
            P("seq", "mp"),
            P("seq", "mp"),
            P("seq", "mp"),
            P("seq", "mp"),
            P(),
            P(),
            P(),
            P(None, "mp"),
            P(None, "mp", None),
            P("mp", None),
            P(None, None, "mp"),
            P("mp", None),
        ),
        out_specs=(
            P("seq", "mp"),
            P("seq", "mp"),
            P("seq", "mp"),
            P("seq", "mp"),
            P("seq", "mp"),
            P(None, "seq", None),
            P("mp", "seq"),
        ),
        check_vma=False,
    )
```
